32 devices in a mesh: ctx: 2 (over core), exp: 16 (over z, y, x).
Axes of the slice: x: 2, y: 2, z: 4, core: 2. Of those that a mesh axis runs over, the one named last changes fastest.
Arguments:
- queries: bfloat16 [512, 36864], P('ctx', 'exp'), may hold values from -400 to 400
- latent: bfloat16 [512, 576], P('ctx'), may hold values from -6.5 to 6.5
- value_up: bfloat16 [64, 512, 128], P('exp'), may hold values from -1 to 1
- out_proj: bfloat16 [8192, 7168], P('exp'), may hold values from -0.0625 to 0.0625
- residual: bfloat16 [512, 7168], P(('ctx', 'exp')), may hold values from -3 to 3
- norm_gain: bfloat16 [7168], replicated, may hold values from 0.5 to 1.5
- routes: int32 [512, 8], P(('ctx', 'exp')), may hold values from 0 to 15, all different within a row; in each aligned block of 16 rows (0 to 15, 16 to 31, ...) at most 12 rows name the same one
- gates: float32 [512, 8], P(('ctx', 'exp')), may hold values from 0.1 to 1
- w_gate: bfloat16 [16, 7168, 1024], P('exp', None, 'ctx'), may hold values from -0.0625 to 0.0625
- w_up: bfloat16 [16, 7168, 1024], P('exp', None, 'ctx'), may hold values from -0.0625 to 0.0625
- w_down: bfloat16 [16, 1024, 7168], P('exp', 'ctx'), may hold values from -0.1875 to 0.1875
Outputs:
- hidden_state: bfloat16 [512, 7168], P(('ctx', 'exp'))
- expert_out: bfloat16 [2, 16, 16, 12, 7168], P('ctx', 'exp')
The draws below stay inside these ranges and needn't reach their ends.
Inputs may be any that keep to these rules, and one draw needn't show every extreme that they name: `routes`: each token names 8 different experts. In every aligned block of 16 tokens no expert is named by more than 12 tokens, and in every draw some block names some expert exactly 12 times.
All inputs are finite; a program needn't handle non-finite values.
Results may differ from the reference program's by a relative error of at most 0.03.
Values may be sent and summed in bfloat16 or wider, within the bound.
No kernel may reach another device: no remote copies, remote signals or barrier semaphores. Data moves between devices by JAX's collectives and lax.ppermute only.
A program may use at most 128 MiB of HBM per device.

```python
import math
import jax
import jax.numpy as jnp
import numpy as np
from jax import lax

MODEL_WIDTH = 7168
LATENT = 512
HEAD_V = 128
QK = 576
HEADS = 64
EXP_HIDDEN = 1024
TOP = 8
SLABS = 2
SENDERS = 16
EXPERTS = 16
ROWS_DEV = 16
SEQ = 512
WINDOW = 256
EXPERT_SLOTS = 12


def shared_fields(key):
    base_key = jax.random.fold_in(key, 7)
    key_lat, key_query = jax.random.split(base_key, 2)
    latent = jnp.clip(jax.random.normal(key_lat, (SEQ, QK), jnp.float32), -6.0, 6.0)
    queries = jnp.clip(jax.random.normal(key_query, (SEQ, HEADS, QK), jnp.float32), -6.0, 6.0)
    return (queries.reshape(SEQ, HEADS * QK), latent)


def draw_queries(key, part):
    return shared_fields(key)[0].astype(jnp.bfloat16)


def draw_latent(key, part):
    return shared_fields(key)[1].astype(jnp.bfloat16)


def shard_levels(own_key, extent, shards, low, top_value):
    factor_of = 1.0
    for dim, blocks in shards:
        draws = jax.random.uniform(jax.random.fold_in(jax.random.fold_in(own_key, 6), dim), (blocks,), jnp.float32, low / len(shards), top_value / len(shards))
        factor_of = factor_of * jnp.repeat(jnp.exp(draws), extent[dim] // blocks).reshape((-1,) + (1,) * (len(extent) - 1 - dim))
    return factor_of


def assign_block(own_key, own, number, rows, number_of, top, limit, slope):
    sequence = jax.random.permutation(own_key, number_of)
    crowded, common = portions_of(number_of, rows * top, limit, slope, True), portions_of(number_of, rows * top, limit, slope, False)
    places = jnp.arange(number_of)

    def named(tallies, offset_by):
        used = int((tallies > 0).sum())
        fixed = max(1, used // 4)
        passed = fixed + (places - fixed + offset_by * (used - fixed)) % max(1, number_of - fixed)
        return jnp.zeros((number_of,), jnp.int32).at[sequence[jnp.where(places < fixed, places, passed)]].set(jnp.asarray(tallies, jnp.int32))

    tallies = jnp.where(number % 4 == 0, named(crowded, number // 4), named(common, number - number // 4 - 1))
    mixed = jax.random.permutation(jax.random.fold_in(own, 3), number_of)
    source_of, sink = mixed[0:number_of // 2 * 2:2], mixed[1:number_of // 2 * 2:2]
    room = jnp.minimum(tallies[source_of] - 1, limit - tallies[sink]) // 2
    room = jnp.where((source_of == sequence[0]) | (sink == sequence[0]) | (tallies[sink] == 0), 0, jnp.maximum(room, 0))
    passed = jax.random.randint(jax.random.fold_in(own, 4), (number_of // 2,), 0, 1 << 20) % (room + 1)
    tallies = tallies.at[source_of].add(-passed).at[sink].add(passed)
    labels = jnp.searchsorted(jnp.cumsum(tallies), jnp.arange(rows * top), side="right").astype(jnp.int32)
    grid = labels.reshape(top, rows).T
    grid = grid[jax.random.permutation(jax.random.fold_in(own, 1), rows)]
    offset_by = jax.random.randint(jax.random.fold_in(own, 2), (rows, 1), 0, top)
    return jnp.take_along_axis(grid, (jnp.arange(top)[None, :] + offset_by) % top, axis=1)


def portions_of(amount, total, most, skew, full):
    weights = [(1 << 20) // math.isqrt(rank ** skew) + 1 for rank in range(1, amount + 1)]
    largest = most if full else min(most, max(-(-total // amount), total * weights[0] // sum(weights)))
    least = 1 if total - largest >= amount - 1 else 0
    holding, surplus = [largest] + [least] * (amount - 1), total - largest - least * (amount - 1)
    while surplus > 0:
        free = [i for i in range(1, amount) if holding[i] < largest] or [i for i in range(1, amount) if holding[i] < most]
        pool, left = sum([weights[i] for i in free]), surplus
        for i in free:
            addition = min(most - holding[i], max(1, left * weights[i] // pool), surplus)
            holding[i] = holding[i] + addition
            surplus = surplus - addition
    return np.array(holding)


def centred(own_key, shape, deviation, bound, shards=(), kind=jnp.bfloat16):
    loudness = shard_levels(own_key, shape, shards, -0.22, 0.18) if shards else 1.0
    entries = jax.random.normal(own_key, shape, jnp.float32) * deviation * loudness
    return jnp.minimum(jnp.maximum(entries, -bound), bound).astype(kind)


def setup_inputs(seed: int = 0) -> dict:
    seeds = jax.random.split(jax.random.key(seed), 12)
    queries = draw_queries(jax.random.fold_in(seeds[11], 71), 0)
    latent = draw_latent(jax.random.fold_in(seeds[11], 71), 0)
    value_up = centred(seeds[2], (HEADS, LATENT, HEAD_V), (LATENT // 16) ** -0.5, 1.0, ((0, 16),))
    out_proj = centred(seeds[3], (HEADS * HEAD_V, MODEL_WIDTH), (HEADS * HEAD_V) ** -0.5, 0.0625, ((0, 16),))
    residual = centred(seeds[4], (SEQ, MODEL_WIDTH), 0.5, 3.0, ((0, 32),))
    norm_gain = jnp.clip(1.0 + 0.1 * jax.random.normal(seeds[5], (MODEL_WIDTH,), jnp.float32), 0.5, 1.5).astype(jnp.bfloat16)
    routes_keys = jax.random.split(jax.random.fold_in(seeds[6], 1), SEQ // ROWS_DEV)
    routes_turns = jax.random.permutation(jax.random.fold_in(seeds[6], 3), SEQ // ROWS_DEV)
    routes = jax.vmap(lambda own, number: assign_block(jax.random.fold_in(seeds[6], 2), own, number, ROWS_DEV, EXPERTS, TOP, EXPERT_SLOTS, 2))(routes_keys, routes_turns).reshape((SEQ, TOP))
    gates = jnp.clip(0.1 + 0.9 * jax.random.uniform(seeds[7], (SEQ, TOP), jnp.float32) ** shard_levels(seeds[7], (SEQ, TOP), ((0, 32),), -0.2, 0.2), 0.1, 1.0)
    w_gate = centred(seeds[8], (EXPERTS, MODEL_WIDTH, EXP_HIDDEN), MODEL_WIDTH ** -0.5, 0.0625, ((0, 16), (2, 2)))
    w_up = centred(seeds[9], (EXPERTS, MODEL_WIDTH, EXP_HIDDEN), MODEL_WIDTH ** -0.5, 0.0625, ((0, 16), (2, 2)))
    w_down = centred(seeds[10], (EXPERTS, EXP_HIDDEN, MODEL_WIDTH), EXP_HIDDEN ** -0.5, 0.1875, ((0, 16), (1, 2)))
    return dict(queries=queries, latent=latent, value_up=value_up, out_proj=out_proj, residual=residual, norm_gain=norm_gain, routes=routes, gates=gates, w_gate=w_gate, w_up=w_up, w_down=w_down)


score_scale = 192.0 ** (-0.5)
norm_epsilon = 1e-06

def reference(queries, latent, value_up, out_proj, residual, norm_gain, routes, gates, w_gate, w_up, w_down):
    query_rows = queries.reshape(SEQ, HEADS, QK)
    positions = jnp.arange(SEQ, dtype=jnp.int32)
    visible = (positions[None, :] <= positions[:, None]) & (positions[None, :] > positions[:, None] - WINDOW)
    values = latent[:, :LATENT]

    def one_head(head_index):
        query_head = lax.dynamic_index_in_dim(query_rows, head_index, 1, keepdims=False)
        scores = jnp.dot(query_head, jnp.transpose(latent), preferred_element_type=jnp.float32) * score_scale
        masked = jnp.where(visible, scores, -jnp.inf)
        row_top = lax.optimization_barrier(jnp.max(masked, axis=1, keepdims=True))
        weights = jnp.where(visible, jnp.exp(masked - row_top), 0.0)
        mixed = jnp.dot(weights.astype(jnp.bfloat16), values, preferred_element_type=jnp.float32)
        attended = (mixed / lax.optimization_barrier(jnp.sum(weights, axis=1, keepdims=True))).astype(jnp.bfloat16)
        up_matrix = lax.dynamic_index_in_dim(value_up, head_index, 0, keepdims=False)
        return jnp.dot(attended, up_matrix, preferred_element_type=jnp.float32).astype(jnp.bfloat16)
    per_head = lax.map(one_head, jnp.arange(HEADS, dtype=jnp.int32))
    head_values = jnp.transpose(per_head, (1, 0, 2)).reshape(SEQ, HEADS * HEAD_V)
    projected = jnp.dot(head_values, out_proj, preferred_element_type=jnp.float32)
    hidden_state = (residual.astype(jnp.float32) + projected).astype(jnp.bfloat16)
    widened = hidden_state.astype(jnp.float32)
    normed = (widened * lax.rsqrt(lax.optimization_barrier(jnp.mean(widened * widened, axis=1, keepdims=True)) + norm_epsilon) * norm_gain.astype(jnp.float32)).astype(jnp.bfloat16)
    input_blocks = SEQ // ROWS_DEV
    normalized_blocks = normed.reshape(input_blocks, ROWS_DEV, MODEL_WIDTH).astype(jnp.float32)
    route_blocks = routes.reshape(input_blocks, ROWS_DEV, TOP)
    gate_blocks = gates.reshape(input_blocks, ROWS_DEV, TOP)
    expert_ids = jnp.arange(EXPERTS, dtype=jnp.int32)
    onehot = (route_blocks[:, :, :, None] == expert_ids[None, None, None, :]).astype(jnp.int32).reshape(input_blocks, ROWS_DEV * TOP, EXPERTS)
    earlier = jnp.cumsum(onehot, axis=1) - onehot
    slot_index = lax.optimization_barrier(jnp.sum(earlier * onehot, axis=2)).reshape(input_blocks, ROWS_DEV, TOP)
    slot_ids = jnp.arange(EXPERT_SLOTS, dtype=jnp.int32)
    group_width = EXP_HIDDEN // SLABS

    def one_expert(expert):
        matches = (route_blocks[:, None, :, :] == expert) & (slot_index[:, None, :, :] == slot_ids[None, :, None, None])
        selected_experts = jnp.any(matches, axis=3).astype(jnp.float32)
        incoming_rows = jnp.einsum('cng,cgf->cnf', selected_experts, normalized_blocks).astype(jnp.bfloat16).reshape(input_blocks * EXPERT_SLOTS, MODEL_WIDTH)
        gate_in = lax.optimization_barrier(jnp.sum(jnp.where(matches, gate_blocks[:, None, :, :], 0.0), axis=(2, 3))).astype(jnp.bfloat16).reshape(input_blocks * EXPERT_SLOTS, 1)
        gate_matrix = lax.dynamic_index_in_dim(w_gate, expert, 0, keepdims=False)
        up_matrix = lax.dynamic_index_in_dim(w_up, expert, 0, keepdims=False)
        down_matrix = lax.dynamic_index_in_dim(w_down, expert, 0, keepdims=False)
        gate_values = jnp.dot(incoming_rows, gate_matrix, preferred_element_type=jnp.float32)
        up_values = jnp.dot(incoming_rows, up_matrix, preferred_element_type=jnp.float32)
        act = (jax.nn.silu(gate_values) * up_values).astype(jnp.bfloat16)
        down_sums = jnp.zeros((input_blocks * EXPERT_SLOTS, MODEL_WIDTH), jnp.float32)
        for group_index in range(SLABS):
            lower = group_index * group_width
            group_term = jnp.dot(act[:, lower:lower + group_width], down_matrix[lower:lower + group_width], preferred_element_type=jnp.float32).astype(jnp.bfloat16)
            down_sums = down_sums + group_term.astype(jnp.float32)
        return (gate_in.astype(jnp.float32) * down_sums).astype(jnp.bfloat16).reshape(input_blocks, EXPERT_SLOTS, MODEL_WIDTH)
    results = lax.map(one_expert, expert_ids)
    expert_out = jnp.transpose(results.reshape(EXPERTS, SLABS, SENDERS, EXPERT_SLOTS, MODEL_WIDTH), (1, 0, 2, 3, 4))
    return (hidden_state, expert_out)
```

```python
import functools

import jax
import jax.numpy as jnp
from jax import lax
from jax.experimental import pallas as pl
from jax.experimental.pallas import tpu as pltpu
from jax.sharding import PartitionSpec as P

score_scale = 192.0 ** (-0.5)
norm_epsilon = 1e-06
masked_value = -1e30
LANES = 128
f32 = jnp.float32
bf16 = jnp.bfloat16


def bits_of(count):
    return count.bit_length() - 1


def relative_of(pos, order):
    rel = jnp.zeros_like(pos)
    for i, bit in enumerate(order):
        rel = rel | (((pos >> (len(order) - 1 - i)) & 1) << bit)
    return rel


def order_matrix(rows, block, order, me):
    shift = bits_of(block)
    row = lax.broadcasted_iota(jnp.int32, (rows, rows), 0)
    col = lax.broadcasted_iota(jnp.int32, (rows, rows), 1)
    source = ((relative_of(row >> shift, order) ^ me) << shift) | (row & (block - 1))
    return jnp.where(col == source, 1.0, 0.0).astype(bf16)


def attend_kernel(
    slabs, block, orders, place_ref, q_ref, *refs
):
    keys = refs[:slabs]
    up_ref, wa_ref, wb_ref = refs[slabs : slabs + 3]
    hva_ref, hvb_ref, ka_ref, sa_ref, kb_ref, sb_ref = refs[slabs + 3 : slabs + 9]
    padded_ref, hv_ref = refs[slabs + 9 :]
    heads, latent_width, value_width = up_ref.shape
    qk, slab = keys[0].shape
    rows = q_ref.shape[0]
    span = slab * slabs

    @pl.when(pl.program_id(0) == 0)
    def _():
        here = place_ref[0]
        me = place_ref[1]
        offsets = sorted({(h * qk) % LANES for h in range(heads)})
        padded_ref[...] = jnp.zeros_like(padded_ref)
        for n, offset in enumerate(offsets):
            for k in range(slabs):
                padded_ref[n, offset : offset + qk, k * slab : (k + 1) * slab] = keys[k][...]
        col = lax.broadcasted_iota(jnp.int32, (rows, span), 1)
        key_pos = col
        for k in range(slabs):
            base = lax.rem(here - k + slabs, slabs) * slab
            key_pos = jnp.where(col >= k * slab, col - k * slab + base, key_pos)
        query_pos = lax.broadcasted_iota(jnp.int32, (rows, span), 0) + here * slab
        visible = (key_pos <= query_pos) & (key_pos > query_pos - span // 2)
        for h in range(heads):
            offset = (h * qk) % LANES
            start = h * qk - offset
            width = -(-(offset + qk) // LANES) * LANES
            n = offsets.index(offset)
            scores = (
                jnp.dot(
                    q_ref[:, start : start + width],
                    padded_ref[n, :width, :],
                    preferred_element_type=f32,
                )
                * score_scale
            )
            masked = jnp.where(visible, scores, masked_value)
            top = jnp.max(masked, axis=1, keepdims=True)
            weights = jnp.where(visible, jnp.exp(masked - top), 0.0)
            total = jnp.sum(weights, axis=1, keepdims=True)
            mixed = lax.dot_general(
                weights.astype(bf16),
                padded_ref[0, :latent_width, :],
                (((1,), (1,)), ((), ())),
                preferred_element_type=f32,
            )
            attended = (mixed / total).astype(bf16)
            hv_ref[:, h * value_width : (h + 1) * value_width] = jnp.dot(
                attended, up_ref[h], preferred_element_type=f32
            ).astype(bf16)
        hv = hv_ref[...]
        for out_ref, order in zip((hva_ref, hvb_ref), orders):
            out_ref[...] = jnp.dot(
                order_matrix(rows, block, order, me), hv, preferred_element_type=f32
            ).astype(bf16)

    project(hva_ref, wa_ref, ka_ref, sa_ref)
    project(hvb_ref, wb_ref, kb_ref, sb_ref)


def project(hv_ref, w_ref, keep_ref, send_ref):
    half = keep_ref.shape[0]
    out = jnp.dot(hv_ref[...], w_ref[...], preferred_element_type=f32).astype(bf16)
    keep_ref[...] = out[:half]
    send_ref[...] = out[half:]


def project_kernel(hva_ref, hvb_ref, wa_ref, wb_ref, ka_ref, sa_ref, kb_ref, sb_ref):
    project(hva_ref, wa_ref, ka_ref, sa_ref)
    project(hvb_ref, wb_ref, kb_ref, sb_ref)


def column_tile(columns, most):
    tiles = columns // LANES
    return LANES * max(t for t in range(1, tiles + 1) if tiles % t == 0 and t * LANES <= most)


def project_specs(rows, inner, quarter, tile, chunk):
    steps = quarter // tile
    first = 2 * chunk * steps
    weights = [
        pl.BlockSpec((inner, tile), lambda i, first=first: (0, first + i)),
        pl.BlockSpec((inner, tile), lambda i, first=first + steps: (0, first + i)),
    ]
    outs = [pl.BlockSpec((rows // 2, tile), lambda i: (0, i))] * 4
    shapes = [jax.ShapeDtypeStruct((rows // 2, quarter), bf16)] * 4
    return steps, weights, outs, shapes


def whole(shape):
    return pl.BlockSpec(shape, lambda i: (0,) * len(shape))


def attend_project(place, queries, keys, value_up, out_proj, block, orders):
    rows, _ = queries.shape
    heads, _, value_width = value_up.shape
    qk, slab = keys[0].shape
    slabs = len(keys)
    span = slab * slabs
    inner, width = out_proj.shape
    quarter = width // 4
    steps, weights, outs, shapes = project_specs(
        rows, inner, quarter, column_tile(quarter, 896), 0
    )
    offsets = {(h * qk) % LANES for h in range(heads)}
    deep = max(-(-(o + qk) // LANES) * LANES for o in offsets)
    flops = 2 * rows * (heads * span * 2 * qk + inner * (width // 2))
    return pl.pallas_call(
        functools.partial(attend_kernel, slabs, block, orders),
        grid=(steps,),
        in_specs=[
            pl.BlockSpec(memory_space=pltpu.SMEM),
            whole(queries.shape),
            *[whole(k.shape) for k in keys],
            whole(value_up.shape),
            *weights,
        ],
        out_specs=[whole((rows, inner))] * 2 + outs,
        out_shape=[jax.ShapeDtypeStruct((rows, inner), bf16)] * 2 + shapes,
        scratch_shapes=[
            pltpu.VMEM((len(offsets), deep, span), bf16),
            pltpu.VMEM((rows, inner), bf16),
        ],
        compiler_params=pltpu.CompilerParams(vmem_limit_bytes=40 << 20),
        cost_estimate=pl.CostEstimate(
            flops=flops,
            bytes_accessed=inner * width + rows * width + queries.size * 2,
            transcendentals=rows * span * heads,
        ),
        name="attend_project",
    )(place, queries, *keys, value_up, out_proj, out_proj)


def project_more(hva, hvb, out_proj, chunk):
    rows, inner = hva.shape
    width = out_proj.shape[1]
    quarter = width // 4
    steps, weights, outs, shapes = project_specs(
        rows, inner, quarter, column_tile(quarter, 896), chunk
    )
    return pl.pallas_call(
        project_kernel,
        grid=(steps,),
        in_specs=[whole(hva.shape), whole(hvb.shape), *weights],
        out_specs=outs,
        out_shape=shapes,
        compiler_params=pltpu.CompilerParams(vmem_limit_bytes=32 << 20),
        cost_estimate=pl.CostEstimate(
            flops=rows * inner * width,
            bytes_accessed=inner * width + rows * width,
            transcendentals=0,
        ),
        name="project_more",
    )(hva, hvb, out_proj, out_proj)


def place_rows(quarter_rows, columns, deep, a_refs, b_refs, x_ref):
    a_low, a_high = a_refs
    b_low, b_high = b_refs
    q = quarter_rows
    pieces = [
        (a_low, 0, 2 * q, 0, 0),
        (a_high, 0, 2 * q, 2 * q, 0),
        (b_low, 0, q, 0, columns),
        (b_low, q, q, 2 * q, columns),
        (b_high, 0, q, q, columns),
        (b_high, q, q, 3 * q, columns),
    ]
    for ref, source, count, target, first in pieces:
        done = 0
        while done < columns:
            tile, inside = divmod(first + done, deep)
            size = min(deep - inside, columns - done)
            x_ref[tile, target : target + count, inside : inside + size] = ref[
                source : source + count, done : done + size
            ]
            done += size


def gate_up_step(x, gates, ups, acc_ref, base_ref):
    for n, group in enumerate((gates, ups)):
        for p, w_ref in enumerate(group):
            wide = w_ref.shape[2]
            cols = slice(p * wide, (p + 1) * wide)
            acc_ref[n, :, cols] = base_ref[n, :, cols] + jnp.dot(
                x, w_ref[0], preferred_element_type=f32
            )


def gate_up_kernel(slabs, quarter_rows, columns, deep, *refs):
    a_refs, b_refs = refs[:2], refs[2:4]
    gates, ups = refs[4 : 4 + slabs], refs[4 + slabs : 4 + 2 * slabs]
    acc_ref, x_ref = refs[4 + 2 * slabs :]

    @pl.when(pl.program_id(0) == 0)
    def _():
        place_rows(quarter_rows, columns, deep, a_refs, b_refs, x_ref)
        acc_ref[...] = jnp.zeros_like(acc_ref)

    gate_up_step(x_ref[pl.program_id(0)], gates, ups, acc_ref, acc_ref)


def finish_kernel(
    slabs, quarter_rows, columns, deep, steps, block, order, top, senders, slots, place_ref, *refs
):
    a_refs, b_refs = refs[:2], refs[2:4]
    base_ref = refs[4]
    gates, ups = refs[5 : 5 + slabs], refs[5 + slabs : 5 + 2 * slabs]
    downs = refs[5 + 2 * slabs : 5 + 3 * slabs]
    out_ref, x_ref, acc_ref, act_ref, gate_ref = refs[5 + 3 * slabs :]
    step = pl.program_id(0)
    rows = 4 * quarter_rows
    q = quarter_rows

    @pl.when(step == 0)
    def _():
        place_rows(quarter_rows, columns, deep, a_refs, b_refs, x_ref)
        gate_up_step(x_ref[0], gates, ups, acc_ref, base_ref)

    @pl.when((step > 0) & (step < steps))
    def _():
        gate_up_step(x_ref[step], gates, ups, acc_ref, acc_ref)

    @pl.when(step == steps - 1)
    def _():
        me = place_ref[1]
        b_low, b_high = b_refs
        meta = jnp.concatenate(
            [b_low[:q, columns:], b_high[:q, columns:], b_low[q:, columns:], b_high[q:, columns:]],
            axis=0,
        ).astype(f32)
        lane = lax.broadcasted_iota(jnp.int32, (rows, LANES), 1)
        named = (lane < top) & (meta == me.astype(f32))
        hit = jnp.max(jnp.where(named, 1.0, 0.0), axis=1, keepdims=True)
        aligned = pltpu.roll(meta, LANES - top, 1)
        gate = jnp.sum(jnp.where(named, aligned, 0.0), axis=1, keepdims=True)
        inverse = jnp.sum(
            jnp.where((lane == 2 * top) | (lane == 2 * top + 1), meta, 0.0), axis=1, keepdims=True
        )
        r = lax.broadcasted_iota(jnp.int32, (rows, rows), 0)
        c = lax.broadcasted_iota(jnp.int32, (rows, rows), 1)
        shift = bits_of(block)
        before = jnp.where(((r >> shift) == (c >> shift)) & (c < r), 1.0, 0.0).astype(bf16)
        hits = jnp.broadcast_to(hit, (rows, LANES))
        slot = jnp.dot(before, hits.astype(bf16), preferred_element_type=f32)
        pos = lax.broadcasted_iota(jnp.int32, (rows, LANES), 0) >> shift
        sender = (relative_of(pos, order) ^ me).astype(f32)
        target = jnp.where(hits > 0.5, slot * senders + sender, -1.0)
        target_row = jnp.transpose(target)[:1, :]
        wanted = lax.broadcasted_iota(jnp.int32, (slots, rows), 0).astype(f32)
        select = jnp.where(wanted == target_row, 1.0, 0.0).astype(bf16)
        gate_ref[...] = jnp.dot(
            select,
            jnp.broadcast_to(gate, (rows, LANES)).astype(bf16),
            preferred_element_type=f32,
        )
        gated = acc_ref[0] * inverse
        upped = acc_ref[1] * inverse
        act = (gated / (1.0 + jnp.exp(-gated)) * upped).astype(bf16)
        act_ref[...] = jnp.dot(select, act, preferred_element_type=f32).astype(bf16)

    @pl.when(step >= steps)
    def _():
        total = None
        for p, w_ref in enumerate(downs):
            part = w_ref.shape[1]
            term = jnp.dot(
                act_ref[:, p * part : (p + 1) * part], w_ref[0], preferred_element_type=f32
            )
            total = term if total is None else total + term
        out_ref[...] = (total * gate_ref[:, :1]).astype(bf16)


def gate_up(a, b, gates, ups, deep):
    half, columns = a[0].shape
    rows = 2 * half
    hidden = sum(w.shape[2] for w in gates)
    steps = 2 * columns // deep
    spec = [pl.BlockSpec((1, deep, w.shape[2]), lambda i: (0, i, 0)) for w in gates + ups]
    return pl.pallas_call(
        functools.partial(gate_up_kernel, len(gates), rows // 4, columns, deep),
        grid=(steps,),
        in_specs=[whole(v.shape) for v in a + b] + spec,
        out_specs=whole((2, rows, hidden)),
        out_shape=jax.ShapeDtypeStruct((2, rows, hidden), f32),
        scratch_shapes=[pltpu.VMEM((steps, rows, deep), bf16)],
        compiler_params=pltpu.CompilerParams(vmem_limit_bytes=40 << 20),
        cost_estimate=pl.CostEstimate(
            flops=8 * rows * columns * hidden,
            bytes_accessed=8 * columns * hidden + 8 * rows * hidden,
            transcendentals=0,
        ),
        name="gate_up",
    )(*a, *b, *gates, *ups)


def finish(place, a, b, base, gates, ups, downs, deep, block, order, top, senders, capacity):
    half, columns = a[0].shape
    rows = 2 * half
    hidden = sum(w.shape[2] for w in gates)
    width = downs[0].shape[2]
    steps = 2 * columns // deep
    tile = column_tile(width, 1024)
    more = width // tile
    slots = senders * capacity
    last = steps - 1
    spec = [
        pl.BlockSpec((1, deep, w.shape[2]), lambda i: (0, steps + jnp.minimum(i, last), 0))
        for w in gates + ups
    ]
    spec += [
        pl.BlockSpec((1, w.shape[1], tile), lambda i: (0, 0, jnp.maximum(i - steps, 0)))
        for w in downs
    ]
    return pl.pallas_call(
        functools.partial(
            finish_kernel, len(gates), rows // 4, columns, deep, steps, block, order, top, senders, slots
        ),
        grid=(steps + more,),
        in_specs=[pl.BlockSpec(memory_space=pltpu.SMEM)]
        + [whole(v.shape) for v in a + b]
        + [whole(base.shape)]
        + spec,
        out_specs=pl.BlockSpec((slots, tile), lambda i: (0, jnp.maximum(i - steps, 0))),
        out_shape=jax.ShapeDtypeStruct((slots, width), bf16),
        scratch_shapes=[
            pltpu.VMEM((steps, rows, deep), bf16),
            pltpu.VMEM((2, rows, hidden), f32),
            pltpu.VMEM((slots, hidden), bf16),
            pltpu.VMEM((slots, LANES), f32),
        ],
        compiler_params=pltpu.CompilerParams(vmem_limit_bytes=48 << 20),
        cost_estimate=pl.CostEstimate(
            flops=8 * rows * columns * hidden + 2 * slots * hidden * width,
            bytes_accessed=8 * columns * hidden + 2 * hidden * width + 2 * slots * width,
            transcendentals=rows * hidden,
        ),
        name="finish",
    )(place, *a, *b, base, *gates, *ups, *downs)


def add(a, b):
    return (a.astype(f32) + b.astype(f32)).astype(bf16)


def swap(value, bit, count):
    return lax.ppermute(value, "exp", [(i, i ^ (1 << bit)) for i in range(count)])


def shifted(value, count):
    return [value] + [
        lax.ppermute(value, "ctx", [(i, (i + k) % count) for i in range(count)])
        for k in range(1, count)
    ]


def scatter_sum(parts, count, bits):
    keep_a, send_a, keep_b, send_b = parts
    got_a, got_b = swap(send_a, 0, count), swap(send_b, 1, count)
    half = keep_a.shape[0] // 2
    next_a = add(keep_a[half:], got_a[half:])
    next_b = add(keep_b[half:], got_b[half:])
    got_a2, got_b2 = swap(next_a, 1, count), swap(next_b, 0, count)
    keep_a = add(keep_a[:half], got_a[:half])
    keep_b = add(keep_b[:half], got_b[:half])
    keep, got = (
        jnp.concatenate([keep_a, keep_b], axis=1),
        jnp.concatenate([got_a2, got_b2], axis=1),
    )
    for bit in range(2, bits):
        half = keep.shape[0] // 2
        arrived = swap(add(keep[half:], got[half:]), bit, count)
        keep, got = add(keep[:half], got[:half]), arrived
    return keep, got


def gather_rows(rows, split, count, bits):
    for bit in range(bits - 1, 1, -1):
        rows = jnp.concatenate([rows, swap(rows, bit, count)], axis=0)
    out = []
    for part, (first, second) in ((rows[:, :split], (1, 0)), (rows[:, split:], (0, 1))):
        low = jnp.concatenate([part, swap(part, first, count)], axis=0)
        out.append([low, swap(low, second, count)])
    return out


def body(
    queries, latent, value_up, out_proj, residual, norm_gain, routes, gates, w_gate, w_up, w_down
):
    slabs = lax.axis_size("ctx")
    senders = lax.axis_size("exp")
    bits = bits_of(senders)
    block, width = residual.shape
    top = routes.shape[1]
    expert_count = senders * w_gate.shape[0]
    capacity = max(2, 3 * block * top // (2 * expert_count))
    orders = (list(range(bits)), [1, 0, *range(2, bits)])
    place = jnp.stack([lax.axis_index("ctx"), lax.axis_index("exp")]).astype(jnp.int32)

    keys = shifted(latent.T, slabs)
    gate_parts = shifted(w_gate, slabs)
    up_parts = shifted(w_up, slabs)
    down_parts = shifted(w_down, slabs)

    hva, hvb, *parts = attend_project(
        place, queries, keys, value_up, out_proj, block, orders
    )
    chunks = [parts, project_more(hva, hvb, out_proj, 1)]
    half_width = width // 2
    gain = norm_gain.astype(f32)
    hidden, payload, squares = [], [], 0.0
    for c, terms in enumerate(chunks):
        keep, got = scatter_sum(terms, senders, bits)
        cols = slice(c * half_width, (c + 1) * half_width)
        rows = (residual[:, cols].astype(f32) + (keep.astype(f32) + got.astype(f32))).astype(bf16)
        wide = rows.astype(f32)
        squares = squares + jnp.sum(wide * wide, axis=1, keepdims=True)
        hidden.append(rows)
        payload.append((wide * gain[None, cols]).astype(bf16))
    inverse = lax.rsqrt(squares / width + norm_epsilon)
    coarse = lax.reduce_precision(inverse, 8, 7)
    meta = jnp.concatenate(
        [
            routes.astype(bf16),
            gates.astype(bf16),
            coarse.astype(bf16),
            (inverse - coarse).astype(bf16),
            jnp.zeros((block, LANES - 2 * top - 2), bf16),
        ],
        axis=1,
    )
    payload[1] = jnp.concatenate([payload[1], meta], axis=1)

    deep = column_tile(half_width, 512)
    a, b = gather_rows(payload[0], half_width // 2, senders, bits)
    base = gate_up(a, b, gate_parts, up_parts, deep)
    a, b = gather_rows(payload[1], half_width // 2, senders, bits)
    slots = finish(
        place, a, b, base, gate_parts, up_parts, down_parts, deep, block, orders[0], top, senders, capacity
    )
    expert_out = slots.reshape(capacity, senders, width).transpose(1, 0, 2)[None, None]
    return jnp.concatenate(hidden, axis=1), expert_out


def solution(mesh):
    placed = (
        P("ctx", "exp"),
        P("ctx", None),
        P("exp", None, None),
        P("exp", None),
        P(("ctx", "exp"), None),
        P(),
        P(("ctx", "exp"), None),
        P(("ctx", "exp"), None),
        P("exp", None, "ctx"),
        P("exp", None, "ctx"),
        P("exp", "ctx", None),
    )
    return jax.shard_map(
        body,
        mesh=mesh,
        in_specs=placed,
        out_specs=(P(("ctx", "exp"), None), P("ctx", "exp", None, None, None)),
        check_vma=False,
    )
```

```python
import functools

import jax
import jax.numpy as jnp
from jax import lax
from jax.experimental import pallas as pl
from jax.experimental.pallas import tpu as pltpu
from jax.sharding import PartitionSpec as P

score_scale = 192.0 ** (-0.5)
norm_epsilon = 1e-06
masked_value = -1e30
LANES = 128
f32 = jnp.float32
bf16 = jnp.bfloat16


def bits_of(count):
    return count.bit_length() - 1


def relative_of(pos, order):
    rel = jnp.zeros_like(pos)
    for i, bit in enumerate(order):
        rel = rel | (((pos >> (len(order) - 1 - i)) & 1) << bit)
    return rel


def order_matrix(rows, block, order, me):
    shift = bits_of(block)
    row = lax.broadcasted_iota(jnp.int32, (rows, rows), 0)
    col = lax.broadcasted_iota(jnp.int32, (rows, rows), 1)
    source = ((relative_of(row >> shift, order) ^ me) << shift) | (row & (block - 1))
    return jnp.where(col == source, 1.0, 0.0).astype(bf16)


def attend_kernel(
    slabs, block, orders, place_ref, q_ref, *refs
):
    keys = refs[:slabs]
    up_ref, wa_ref, wb_ref = refs[slabs : slabs + 3]
    hva_ref, hvb_ref, ka_ref, sa_ref, kb_ref, sb_ref = refs[slabs + 3 : slabs + 9]
    padded_ref, hv_ref = refs[slabs + 9 :]
    heads, latent_width, value_width = up_ref.shape
    qk, slab = keys[0].shape
    rows = q_ref.shape[0]
    span = slab * slabs

    @pl.when(pl.program_id(0) == 0)
    def _():
        here = place_ref[0]
        me = place_ref[1]
        offsets = sorted({(h * qk) % LANES for h in range(heads)})
        padded_ref[...] = jnp.zeros_like(padded_ref)
        for n, offset in enumerate(offsets):
            for k in range(slabs):
                padded_ref[n, offset : offset + qk, k * slab : (k + 1) * slab] = keys[k][...]
        col = lax.broadcasted_iota(jnp.int32, (rows, span), 1)
        key_pos = col
        for k in range(slabs):
            base = lax.rem(here - k + slabs, slabs) * slab
            key_pos = jnp.where(col >= k * slab, col - k * slab + base, key_pos)
        query_pos = lax.broadcasted_iota(jnp.int32, (rows, span), 0) + here * slab
        visible = (key_pos <= query_pos) & (key_pos > query_pos - span // 2)
        for h in range(heads):
            offset = (h * qk) % LANES
            start = h * qk - offset
            width = -(-(offset + qk) // LANES) * LANES
            n = offsets.index(offset)
            scores = (
                jnp.dot(
                    q_ref[:, start : start + width],
                    padded_ref[n, :width, :],
                    preferred_element_type=f32,
                )
                * score_scale
            )
            masked = jnp.where(visible, scores, masked_value)
            top = jnp.max(masked, axis=1, keepdims=True)
            weights = jnp.where(visible, jnp.exp(masked - top), 0.0)
            total = jnp.sum(weights, axis=1, keepdims=True)
            mixed = lax.dot_general(
                weights.astype(bf16),
                padded_ref[0, :latent_width, :],
                (((1,), (1,)), ((), ())),
                preferred_element_type=f32,
            )
            attended = (mixed / total).astype(bf16)
            hv_ref[:, h * value_width : (h + 1) * value_width] = jnp.dot(
                attended, up_ref[h], preferred_element_type=f32
            ).astype(bf16)
        hv = hv_ref[...]
        for out_ref, order in zip((hva_ref, hvb_ref), orders):
            out_ref[...] = jnp.dot(
                order_matrix(rows, block, order, me), hv, preferred_element_type=f32
            ).astype(bf16)

    project(hva_ref, wa_ref, ka_ref, sa_ref)
    project(hvb_ref, wb_ref, kb_ref, sb_ref)


def project(hv_ref, w_ref, keep_ref, send_ref):
    half = keep_ref.shape[0]
    out = jnp.dot(hv_ref[...], w_ref[...], preferred_element_type=f32).astype(bf16)
    keep_ref[...] = out[:half]
    send_ref[...] = out[half:]


def project_kernel(hva_ref, hvb_ref, wa_ref, wb_ref, ka_ref, sa_ref, kb_ref, sb_ref):
    project(hva_ref, wa_ref, ka_ref, sa_ref)
    project(hvb_ref, wb_ref, kb_ref, sb_ref)


def in_hbm(value):
    return pltpu.with_memory_space_constraint(value, pltpu.HBM)


def column_tile(columns, most):
    tiles = columns // LANES
    return LANES * max(t for t in range(1, tiles + 1) if tiles % t == 0 and t * LANES <= most)


def project_specs(rows, inner, quarter, tile, chunk):
    steps = quarter // tile
    first = 2 * chunk * steps
    weights = [
        pl.BlockSpec((inner, tile), lambda i, first=first: (0, first + i)),
        pl.BlockSpec((inner, tile), lambda i, first=first + steps: (0, first + i)),
    ]
    outs = [pl.BlockSpec((rows // 2, tile), lambda i: (0, i))] * 4
    shapes = [jax.ShapeDtypeStruct((rows // 2, quarter), bf16)] * 4
    return steps, weights, outs, shapes


def whole(shape):
    return pl.BlockSpec(shape, lambda i: (0,) * len(shape))


def attend_project(place, queries, keys, value_up, out_proj, block, orders):
    rows, _ = queries.shape
    heads, _, value_width = value_up.shape
    qk, slab = keys[0].shape
    slabs = len(keys)
    span = slab * slabs
    inner, width = out_proj.shape
    quarter = width // 4
    steps, weights, outs, shapes = project_specs(
        rows, inner, quarter, column_tile(quarter, 896), 0
    )
    offsets = {(h * qk) % LANES for h in range(heads)}
    deep = max(-(-(o + qk) // LANES) * LANES for o in offsets)
    flops = 2 * rows * (heads * span * 2 * qk + inner * (width // 2))
    return pl.pallas_call(
        functools.partial(attend_kernel, slabs, block, orders),
        grid=(steps,),
        in_specs=[
            pl.BlockSpec(memory_space=pltpu.SMEM),
            whole(queries.shape),
            *[whole(k.shape) for k in keys],
            whole(value_up.shape),
            *weights,
        ],
        out_specs=[whole((rows, inner))] * 2 + outs,
        out_shape=[jax.ShapeDtypeStruct((rows, inner), bf16)] * 2 + shapes,
        scratch_shapes=[
            pltpu.VMEM((len(offsets), deep, span), bf16),
            pltpu.VMEM((rows, inner), bf16),
        ],
        compiler_params=pltpu.CompilerParams(vmem_limit_bytes=24 << 20),
        cost_estimate=pl.CostEstimate(
            flops=flops,
            bytes_accessed=inner * width + rows * width + queries.size * 2,
            transcendentals=rows * span * heads,
        ),
        name="attend_project",
    )(place, in_hbm(queries), *keys, in_hbm(value_up), in_hbm(out_proj), in_hbm(out_proj))


def project_more(hva, hvb, out_proj, chunk):
    rows, inner = hva.shape
    width = out_proj.shape[1]
    quarter = width // 4
    steps, weights, outs, shapes = project_specs(
        rows, inner, quarter, column_tile(quarter, 896), chunk
    )
    return pl.pallas_call(
        project_kernel,
        grid=(steps,),
        in_specs=[whole(hva.shape), whole(hvb.shape), *weights],
        out_specs=outs,
        out_shape=shapes,
        compiler_params=pltpu.CompilerParams(vmem_limit_bytes=16 << 20),
        cost_estimate=pl.CostEstimate(
            flops=rows * inner * width,
            bytes_accessed=inner * width + rows * width,
            transcendentals=0,
        ),
        name="project_more",
    )(hva, hvb, in_hbm(out_proj), in_hbm(out_proj))


def place_rows(quarter_rows, columns, deep, a_refs, b_refs, x_ref):
    a_low, a_high = a_refs
    b_low, b_high = b_refs
    q = quarter_rows
    pieces = [
        (a_low, 0, 2 * q, 0, 0),
        (a_high, 0, 2 * q, 2 * q, 0),
        (b_low, 0, q, 0, columns),
        (b_low, q, q, 2 * q, columns),
        (b_high, 0, q, q, columns),
        (b_high, q, q, 3 * q, columns),
    ]
    for ref, source, count, target, first in pieces:
        done = 0
        while done < columns:
            tile, inside = divmod(first + done, deep)
            size = min(deep - inside, columns - done)
            x_ref[tile, target : target + count, inside : inside + size] = ref[
                source : source + count, done : done + size
            ]
            done += size


def gate_up_step(x, gates, ups, acc_ref, base_ref):
    for n, group in enumerate((gates, ups)):
        for p, w_ref in enumerate(group):
            wide = w_ref.shape[2]
            cols = slice(p * wide, (p + 1) * wide)
            acc_ref[n, :, cols] = base_ref[n, :, cols] + jnp.dot(
                x, w_ref[0], preferred_element_type=f32
            )


def gate_up_kernel(slabs, quarter_rows, columns, deep, *refs):
    a_refs, b_refs = refs[:2], refs[2:4]
    gates, ups = refs[4 : 4 + slabs], refs[4 + slabs : 4 + 2 * slabs]
    acc_ref, x_ref = refs[4 + 2 * slabs :]

    @pl.when(pl.program_id(0) == 0)
    def _():
        place_rows(quarter_rows, columns, deep, a_refs, b_refs, x_ref)
        acc_ref[...] = jnp.zeros_like(acc_ref)

    gate_up_step(x_ref[pl.program_id(0)], gates, ups, acc_ref, acc_ref)


def finish_kernel(
    slabs, quarter_rows, columns, deep, steps, block, order, top, senders, slots, place_ref, *refs
):
    a_refs, b_refs = refs[:2], refs[2:4]
    base_ref = refs[4]
    gates, ups = refs[5 : 5 + slabs], refs[5 + slabs : 5 + 2 * slabs]
    downs = refs[5 + 2 * slabs : 5 + 3 * slabs]
    out_ref, x_ref, acc_ref, act_ref, gate_ref = refs[5 + 3 * slabs :]
    step = pl.program_id(0)
    rows = 4 * quarter_rows
    q = quarter_rows

    @pl.when(step == 0)
    def _():
        place_rows(quarter_rows, columns, deep, a_refs, b_refs, x_ref)
        gate_up_step(x_ref[0], gates, ups, acc_ref, base_ref)

    @pl.when((step > 0) & (step < steps))
    def _():
        gate_up_step(x_ref[step], gates, ups, acc_ref, acc_ref)

    @pl.when(step == steps - 1)
    def _():
        me = place_ref[1]
        b_low, b_high = b_refs
        meta = jnp.concatenate(
            [b_low[:q, columns:], b_high[:q, columns:], b_low[q:, columns:], b_high[q:, columns:]],
            axis=0,
        ).astype(f32)
        lane = lax.broadcasted_iota(jnp.int32, (rows, LANES), 1)
        named = (lane < top) & (meta == me.astype(f32))
        hit = jnp.max(jnp.where(named, 1.0, 0.0), axis=1, keepdims=True)
        aligned = pltpu.roll(meta, LANES - top, 1)
        gate = jnp.sum(jnp.where(named, aligned, 0.0), axis=1, keepdims=True)
        inverse = jnp.sum(
            jnp.where((lane == 2 * top) | (lane == 2 * top + 1), meta, 0.0), axis=1, keepdims=True
        )
        r = lax.broadcasted_iota(jnp.int32, (rows, rows), 0)
        c = lax.broadcasted_iota(jnp.int32, (rows, rows), 1)
        shift = bits_of(block)
        before = jnp.where(((r >> shift) == (c >> shift)) & (c < r), 1.0, 0.0).astype(bf16)
        hits = jnp.broadcast_to(hit, (rows, LANES))
        slot = jnp.dot(before, hits.astype(bf16), preferred_element_type=f32)
        pos = lax.broadcasted_iota(jnp.int32, (rows, LANES), 0) >> shift
        sender = (relative_of(pos, order) ^ me).astype(f32)
        target = jnp.where(hits > 0.5, slot * senders + sender, -1.0)
        target_row = jnp.transpose(target)[:1, :]
        wanted = lax.broadcasted_iota(jnp.int32, (slots, rows), 0).astype(f32)
        select = jnp.where(wanted == target_row, 1.0, 0.0).astype(bf16)
        gate_ref[...] = jnp.dot(
            select,
            jnp.broadcast_to(gate, (rows, LANES)).astype(bf16),
            preferred_element_type=f32,
        )
        gated = acc_ref[0] * inverse
        upped = acc_ref[1] * inverse
        act = (gated / (1.0 + jnp.exp(-gated)) * upped).astype(bf16)
        act_ref[...] = jnp.dot(select, act, preferred_element_type=f32).astype(bf16)

    @pl.when(step >= steps)
    def _():
        total = None
        for p, w_ref in enumerate(downs):
            part = w_ref.shape[1]
            term = jnp.dot(
                act_ref[:, p * part : (p + 1) * part], w_ref[0], preferred_element_type=f32
            )
            total = term if total is None else total + term
        out_ref[...] = (total * gate_ref[:, :1]).astype(bf16)


def gate_up(a, b, gates, ups, deep):
    half, columns = a[0].shape
    rows = 2 * half
    hidden = sum(w.shape[2] for w in gates)
    steps = 2 * columns // deep
    spec = [pl.BlockSpec((1, deep, w.shape[2]), lambda i: (0, i, 0)) for w in gates + ups]
    return pl.pallas_call(
        functools.partial(gate_up_kernel, len(gates), rows // 4, columns, deep),
        grid=(steps,),
        in_specs=[whole(v.shape) for v in a + b] + spec,
        out_specs=whole((2, rows, hidden)),
        out_shape=jax.ShapeDtypeStruct((2, rows, hidden), f32),
        scratch_shapes=[pltpu.VMEM((steps, rows, deep), bf16)],
        compiler_params=pltpu.CompilerParams(vmem_limit_bytes=40 << 20),
        cost_estimate=pl.CostEstimate(
            flops=8 * rows * columns * hidden,
            bytes_accessed=8 * columns * hidden + 8 * rows * hidden,
            transcendentals=0,
        ),
        name="gate_up",
    )(*a, *b, *map(in_hbm, gates + ups))


def finish(place, a, b, base, gates, ups, downs, deep, block, order, top, senders, capacity):
    half, columns = a[0].shape
    rows = 2 * half
    hidden = sum(w.shape[2] for w in gates)
    width = downs[0].shape[2]
    steps = 2 * columns // deep
    tile = column_tile(width, 1792)
    more = width // tile
    slots = senders * capacity
    last = steps - 1
    spec = [
        pl.BlockSpec((1, deep, w.shape[2]), lambda i: (0, steps + jnp.minimum(i, last), 0))
        for w in gates + ups
    ]
    spec += [
        pl.BlockSpec((1, w.shape[1], tile), lambda i: (0, 0, jnp.maximum(i - steps, 0)))
        for w in downs
    ]
    return pl.pallas_call(
        functools.partial(
            finish_kernel, len(gates), rows // 4, columns, deep, steps, block, order, top, senders, slots
        ),
        grid=(steps + more,),
        in_specs=[pl.BlockSpec(memory_space=pltpu.SMEM)]
        + [whole(v.shape) for v in a + b]
        + [whole(base.shape)]
        + spec,
        out_specs=pl.BlockSpec((slots, tile), lambda i: (0, jnp.maximum(i - steps, 0))),
        out_shape=jax.ShapeDtypeStruct((slots, width), bf16),
        scratch_shapes=[
            pltpu.VMEM((steps, rows, deep), bf16),
            pltpu.VMEM((2, rows, hidden), f32),
            pltpu.VMEM((slots, hidden), bf16),
            pltpu.VMEM((slots, LANES), f32),
        ],
        compiler_params=pltpu.CompilerParams(vmem_limit_bytes=44 << 20),
        cost_estimate=pl.CostEstimate(
            flops=8 * rows * columns * hidden + 2 * slots * hidden * width,
            bytes_accessed=8 * columns * hidden + 2 * hidden * width + 2 * slots * width,
            transcendentals=rows * hidden,
        ),
        name="finish",
    )(place, *a, *b, base, *map(in_hbm, gates + ups + downs))


def add(a, b):
    return (a.astype(f32) + b.astype(f32)).astype(bf16)


def swap(value, bit, count):
    return lax.ppermute(value, "exp", [(i, i ^ (1 << bit)) for i in range(count)])


def shifted(value, count):
    return [value] + [
        lax.ppermute(value, "ctx", [(i, (i + k) % count) for i in range(count)])
        for k in range(1, count)
    ]


def tie(*values):
    return lax.optimization_barrier(values)


def first_swap(parts, count):
    _, send_a, _, send_b = parts
    return swap(send_a, 0, count), swap(send_b, 1, count)


def second_swap(parts, got, count):
    keep_a, _, keep_b, _ = parts
    got_a, got_b = got
    half = keep_a.shape[0] // 2
    next_a = add(keep_a[half:], got_a[half:])
    next_b = add(keep_b[half:], got_b[half:])
    got_a2, got_b2 = swap(next_a, 1, count), swap(next_b, 0, count)
    keep_a = add(keep_a[:half], got_a[:half])
    keep_b = add(keep_b[:half], got_b[:half])
    return keep_a, keep_b, got_a2, got_b2


def last_swaps(terms, count, bits):
    keep_a, keep_b, got_a, got_b = terms
    keep = jnp.concatenate([keep_a, keep_b], axis=1)
    got = jnp.concatenate([got_a, got_b], axis=1)
    for bit in range(2, bits):
        half = keep.shape[0] // 2
        arrived = swap(add(keep[half:], got[half:]), bit, count)
        keep, got = add(keep[:half], got[:half]), arrived
    return keep, got


def gather_rows(rows, split, count, bits):
    for bit in range(bits - 1, 1, -1):
        rows = jnp.concatenate([rows, swap(rows, bit, count)], axis=0)
    out = []
    for part, (first, second) in ((rows[:, :split], (1, 0)), (rows[:, split:], (0, 1))):
        low = jnp.concatenate([part, swap(part, first, count)], axis=0)
        out.append([low, swap(low, second, count)])
    return out


def body(
    queries, latent, value_up, out_proj, residual, norm_gain, routes, gates, w_gate, w_up, w_down
):
    slabs = lax.axis_size("ctx")
    senders = lax.axis_size("exp")
    bits = bits_of(senders)
    block, width = residual.shape
    top = routes.shape[1]
    expert_count = senders * w_gate.shape[0]
    capacity = max(2, 3 * block * top // (2 * expert_count))
    orders = (list(range(bits)), [1, 0, *range(2, bits)])
    place = jnp.stack([lax.axis_index("ctx"), lax.axis_index("exp")]).astype(jnp.int32)

    keys = shifted(latent.T, slabs)
    gate_parts = shifted(w_gate, slabs)

    hva, hvb, *parts = attend_project(
        place, queries, keys, value_up, out_proj, block, orders
    )
    more = project_more(hva, hvb, out_proj, 1)
    got = first_swap(parts, senders)
    got, more, gate_parts, w_up = tie(got, more, gate_parts, w_up)
    up_parts = shifted(w_up, slabs)
    terms = [second_swap(parts, got, senders)]
    got = first_swap(more, senders)
    got, terms[0], up_parts, w_down = tie(got, terms[0], up_parts, w_down)
    down_parts = shifted(w_down, slabs)
    terms.append(second_swap(more, got, senders))
    sums = [last_swaps(t, senders, bits) for t in terms]
    sums[1], down_parts = tie(sums[1], down_parts)
    half_width = width // 2
    gain = norm_gain.astype(f32)
    hidden, payload, squares = [], [], 0.0
    for c, (keep, got) in enumerate(sums):
        cols = slice(c * half_width, (c + 1) * half_width)
        rows = (residual[:, cols].astype(f32) + (keep.astype(f32) + got.astype(f32))).astype(bf16)
        wide = rows.astype(f32)
        squares = squares + jnp.sum(wide * wide, axis=1, keepdims=True)
        hidden.append(rows)
        payload.append((wide * gain[None, cols]).astype(bf16))
    inverse = lax.rsqrt(squares / width + norm_epsilon)
    coarse = lax.reduce_precision(inverse, 8, 7)
    meta = jnp.concatenate(
        [
            routes.astype(bf16),
            gates.astype(bf16),
            coarse.astype(bf16),
            (inverse - coarse).astype(bf16),
            jnp.zeros((block, LANES - 2 * top - 2), bf16),
        ],
        axis=1,
    )
    payload[1] = jnp.concatenate([payload[1], meta], axis=1)

    deep = column_tile(half_width, 1792)
    a, b = gather_rows(payload[0], half_width // 2, senders, bits)
    base = gate_up(a, b, gate_parts, up_parts, deep)
    a, b = gather_rows(payload[1], half_width // 2, senders, bits)
    slots = finish(
        place, a, b, base, gate_parts, up_parts, down_parts, deep, block, orders[0], top, senders, capacity
    )
    expert_out = slots.reshape(capacity, senders, width).transpose(1, 0, 2)[None, None]
    return jnp.concatenate(hidden, axis=1), expert_out


def solution(mesh):
    placed = (
        P("ctx", "exp"),
        P("ctx", None),
        P("exp", None, None),
        P("exp", None),
        P(("ctx", "exp"), None),
        P(),
        P(("ctx", "exp"), None),
        P(("ctx", "exp"), None),
        P("exp", None, "ctx"),
        P("exp", None, "ctx"),
        P("exp", "ctx", None),
    )
    return jax.shard_map(
        body,
        mesh=mesh,
        in_specs=placed,
        out_specs=(P(("ctx", "exp"), None), P("ctx", "exp", None, None, None)),
        check_vma=False,
    )
```

```python
import functools

import jax
import jax.numpy as jnp
from jax import lax
from jax.experimental import pallas as pl
from jax.experimental.pallas import tpu as pltpu
from jax.sharding import PartitionSpec as P

score_scale = 192.0 ** (-0.5)
norm_epsilon = 1e-06
masked_value = -1e30
LANES = 128
f32 = jnp.float32
bf16 = jnp.bfloat16


def bits_of(count):
    return count.bit_length() - 1


def relative_of(pos, order):
    rel = jnp.zeros_like(pos)
    for i, bit in enumerate(order):
        rel = rel | (((pos >> (len(order) - 1 - i)) & 1) << bit)
    return rel


def order_matrix(rows, block, order, me):
    shift = bits_of(block)
    row = lax.broadcasted_iota(jnp.int32, (rows, rows), 0)
    col = lax.broadcasted_iota(jnp.int32, (rows, rows), 1)
    source = ((relative_of(row >> shift, order) ^ me) << shift) | (row & (block - 1))
    return jnp.where(col == source, 1.0, 0.0).astype(bf16)


def attend_kernel(
    slabs, block, orders, place_ref, q_ref, *refs
):
    keys = refs[:slabs]
    up_ref, wa_ref, wb_ref = refs[slabs : slabs + 3]
    hva_ref, hvb_ref, ka_ref, sa_ref, kb_ref, sb_ref = refs[slabs + 3 : slabs + 9]
    padded_ref, hv_ref = refs[slabs + 9 :]
    heads, latent_width, value_width = up_ref.shape
    qk, slab = keys[0].shape
    rows = q_ref.shape[0]
    span = slab * slabs

    @pl.when(pl.program_id(0) == 0)
    def _():
        here = place_ref[0]
        me = place_ref[1]
        offsets = sorted({(h * qk) % LANES for h in range(heads)})
        padded_ref[...] = jnp.zeros_like(padded_ref)
        for n, offset in enumerate(offsets):
            for k in range(slabs):
                padded_ref[n, offset : offset + qk, k * slab : (k + 1) * slab] = keys[k][...]
        col = lax.broadcasted_iota(jnp.int32, (rows, span), 1)
        key_pos = col
        for k in range(slabs):
            base = lax.rem(here - k + slabs, slabs) * slab
            key_pos = jnp.where(col >= k * slab, col - k * slab + base, key_pos)
        query_pos = lax.broadcasted_iota(jnp.int32, (rows, span), 0) + here * slab
        visible = (key_pos <= query_pos) & (key_pos > query_pos - span // 2)
        for h in range(heads):
            offset = (h * qk) % LANES
            start = h * qk - offset
            width = -(-(offset + qk) // LANES) * LANES
            n = offsets.index(offset)
            scores = (
                jnp.dot(
                    q_ref[:, start : start + width],
                    padded_ref[n, :width, :],
                    preferred_element_type=f32,
                )
                * score_scale
            )
            masked = jnp.where(visible, scores, masked_value)
            top = jnp.max(masked, axis=1, keepdims=True)
            weights = jnp.where(visible, jnp.exp(masked - top), 0.0)
            total = jnp.sum(weights, axis=1, keepdims=True)
            mixed = lax.dot_general(
                weights.astype(bf16),
                padded_ref[0, :latent_width, :],
                (((1,), (1,)), ((), ())),
                preferred_element_type=f32,
            )
            attended = (mixed / total).astype(bf16)
            hv_ref[:, h * value_width : (h + 1) * value_width] = jnp.dot(
                attended, up_ref[h], preferred_element_type=f32
            ).astype(bf16)
        hv = hv_ref[...]
        for out_ref, order in zip((hva_ref, hvb_ref), orders):
            out_ref[...] = jnp.dot(
                order_matrix(rows, block, order, me), hv, preferred_element_type=f32
            ).astype(bf16)

    project(hva_ref, wa_ref, ka_ref, sa_ref)
    project(hvb_ref, wb_ref, kb_ref, sb_ref)


def project(hv_ref, w_ref, keep_ref, send_ref):
    half = keep_ref.shape[0]
    out = jnp.dot(hv_ref[...], w_ref[...], preferred_element_type=f32).astype(bf16)
    keep_ref[...] = out[:half]
    send_ref[...] = out[half:]


def project_kernel(hva_ref, hvb_ref, wa_ref, wb_ref, ka_ref, sa_ref, kb_ref, sb_ref):
    project(hva_ref, wa_ref, ka_ref, sa_ref)
    project(hvb_ref, wb_ref, kb_ref, sb_ref)


def in_hbm(value):
    return pltpu.with_memory_space_constraint(value, pltpu.HBM)


def column_tile(columns, most):
    tiles = columns // LANES
    return LANES * max(t for t in range(1, tiles + 1) if tiles % t == 0 and t * LANES <= most)


def project_specs(rows, inner, quarter, tile, chunk):
    steps = quarter // tile
    first = 2 * chunk * steps
    weights = [
        pl.BlockSpec((inner, tile), lambda i, first=first: (0, first + i)),
        pl.BlockSpec((inner, tile), lambda i, first=first + steps: (0, first + i)),
    ]
    outs = [pl.BlockSpec((rows // 2, tile), lambda i: (0, i))] * 4
    shapes = [jax.ShapeDtypeStruct((rows // 2, quarter), bf16)] * 4
    return steps, weights, outs, shapes


def whole(shape):
    return pl.BlockSpec(shape, lambda i: (0,) * len(shape))


def attend_project(place, queries, keys, value_up, out_proj, block, orders):
    rows, _ = queries.shape
    heads, _, value_width = value_up.shape
    qk, slab = keys[0].shape
    slabs = len(keys)
    span = slab * slabs
    inner, width = out_proj.shape
    quarter = width // 4
    steps, weights, outs, shapes = project_specs(
        rows, inner, quarter, column_tile(quarter, 896), 0
    )
    offsets = {(h * qk) % LANES for h in range(heads)}
    deep = max(-(-(o + qk) // LANES) * LANES for o in offsets)
    flops = 2 * rows * (heads * span * 2 * qk + inner * (width // 2))
    return pl.pallas_call(
        functools.partial(attend_kernel, slabs, block, orders),
        grid=(steps,),
        in_specs=[
            pl.BlockSpec(memory_space=pltpu.SMEM),
            whole(queries.shape),
            *[whole(k.shape) for k in keys],
            whole(value_up.shape),
            *weights,
        ],
        out_specs=[whole((rows, inner))] * 2 + outs,
        out_shape=[jax.ShapeDtypeStruct((rows, inner), bf16)] * 2 + shapes,
        scratch_shapes=[
            pltpu.VMEM((len(offsets), deep, span), bf16),
            pltpu.VMEM((rows, inner), bf16),
        ],
        compiler_params=pltpu.CompilerParams(vmem_limit_bytes=24 << 20),
        cost_estimate=pl.CostEstimate(
            flops=flops,
            bytes_accessed=inner * width + rows * width + queries.size * 2,
            transcendentals=rows * span * heads,
        ),
        name="attend_project",
    )(place, in_hbm(queries), in_hbm(keys[0]), *keys[1:], in_hbm(value_up), in_hbm(out_proj), in_hbm(out_proj))


def project_more(hva, hvb, out_proj, chunk):
    rows, inner = hva.shape
    width = out_proj.shape[1]
    quarter = width // 4
    steps, weights, outs, shapes = project_specs(
        rows, inner, quarter, column_tile(quarter, 896), chunk
    )
    return pl.pallas_call(
        project_kernel,
        grid=(steps,),
        in_specs=[whole(hva.shape), whole(hvb.shape), *weights],
        out_specs=outs,
        out_shape=shapes,
        compiler_params=pltpu.CompilerParams(vmem_limit_bytes=16 << 20),
        cost_estimate=pl.CostEstimate(
            flops=rows * inner * width,
            bytes_accessed=inner * width + rows * width,
            transcendentals=0,
        ),
        name="project_more",
    )(hva, hvb, in_hbm(out_proj), in_hbm(out_proj))


def place_rows(quarter_rows, columns, a_refs, b_refs, x_ref):
    a_low, a_high = a_refs
    b_low, b_high = b_refs
    q = quarter_rows
    for ref, source, count, target, first in (
        (a_low, 0, 2 * q, 0, 0),
        (a_high, 0, 2 * q, 2 * q, 0),
        (b_low, 0, q, 0, columns),
        (b_low, q, q, 2 * q, columns),
        (b_high, 0, q, q, columns),
        (b_high, q, q, 3 * q, columns),
    ):
        x_ref[target : target + count, first : first + columns] = ref[
            source : source + count, :columns
        ]


def weight_copies(pieces, held_ref, sems, first_row):
    deep = held_ref.shape[1]
    copies = []
    for p, w_ref in enumerate(pieces):
        cuts = (0, deep // 2, deep) if p == 0 else (0, deep)
        copies.append(
            [
                (
                    low,
                    high,
                    pltpu.make_async_copy(
                        w_ref.at[0, first_row + low : first_row + high, :],
                        held_ref.at[p, low:high, :],
                        sems.at[p + (n if p == 0 else 1)],
                    ),
                )
                for n, (low, high) in enumerate(zip(cuts, cuts[1:]))
            ]
        )
    return copies


def start_all(copies):
    for group in copies:
        for _, _, copy in group:
            copy.start()


def times_piece(x_ref, held_ref, p, group):
    total = None
    for low, high, copy in group:
        copy.wait()
        term = jnp.dot(x_ref[:, low:high], held_ref[p, low:high, :], preferred_element_type=f32)
        total = term if total is None else total + term
    return total


def gate_up_kernel(slabs, quarter_rows, columns, *refs):
    a_refs, b_refs = refs[:2], refs[2:4]
    pieces = refs[4 : 4 + 2 * slabs]
    acc_ref, x_ref, held_ref, sems = refs[4 + 2 * slabs :]
    copies = weight_copies(pieces, held_ref, sems, 0)
    start_all(copies)
    place_rows(quarter_rows, columns, a_refs, b_refs, x_ref)
    wide = held_ref.shape[2]
    for p, group in enumerate(copies):
        kind, place = divmod(p, slabs)
        acc_ref[kind, :, place * wide : (place + 1) * wide] = times_piece(
            x_ref, held_ref, p, group
        )


def finish_kernel(slabs, quarter_rows, columns, block, order, top, senders, place_ref, *refs):
    a_refs, b_refs = refs[:2], refs[2:4]
    base_ref = refs[4]
    pieces = refs[5 : 5 + 2 * slabs]
    downs = refs[5 + 2 * slabs : 5 + 3 * slabs]
    (out_hbm, x_ref, held_ref, acc_ref, act_ref, down_ref, out_ref, sems, down_sems, out_sems) = refs[
        5 + 3 * slabs :
    ]
    rows = 4 * quarter_rows
    q = quarter_rows
    slots, width = out_ref.shape
    part = downs[0].shape[1]
    wide = held_ref.shape[2]
    tiles = down_sems.shape[0]
    tile = width // tiles
    copies = weight_copies(pieces, held_ref, sems, 2 * columns)
    start_all(copies)
    down_copies = [
        [
            pltpu.make_async_copy(
                w_ref.at[0, :, j * tile : (j + 1) * tile],
                down_ref.at[p * part : (p + 1) * part, j * tile : (j + 1) * tile],
                down_sems.at[j, p],
            )
            for p, w_ref in enumerate(downs)
        ]
        for j in range(tiles)
    ]
    for group in down_copies:
        for copy in group:
            copy.start()
    place_rows(quarter_rows, columns, a_refs, b_refs, x_ref)

    me = place_ref[1]
    b_low, b_high = b_refs
    meta = jnp.concatenate(
        [b_low[:q, columns:], b_high[:q, columns:], b_low[q:, columns:], b_high[q:, columns:]],
        axis=0,
    ).astype(f32)
    lane = lax.broadcasted_iota(jnp.int32, (rows, LANES), 1)
    named = (lane < top) & (meta == me.astype(f32))
    hit = jnp.max(jnp.where(named, 1.0, 0.0), axis=1, keepdims=True)
    aligned = pltpu.roll(meta, LANES - top, 1)
    gate = jnp.sum(jnp.where(named, aligned, 0.0), axis=1, keepdims=True)
    inverse = jnp.sum(
        jnp.where((lane == 2 * top) | (lane == 2 * top + 1), meta, 0.0), axis=1, keepdims=True
    )
    r = lax.broadcasted_iota(jnp.int32, (rows, rows), 0)
    c = lax.broadcasted_iota(jnp.int32, (rows, rows), 1)
    shift = bits_of(block)
    before = jnp.where(((r >> shift) == (c >> shift)) & (c < r), 1.0, 0.0).astype(bf16)
    hits = jnp.broadcast_to(hit, (rows, LANES))
    slot = jnp.dot(before, hits.astype(bf16), preferred_element_type=f32)
    pos = lax.broadcasted_iota(jnp.int32, (rows, LANES), 0) >> shift
    sender = (relative_of(pos, order) ^ me).astype(f32)
    target = jnp.where(hits > 0.5, slot * senders + sender, -1.0)
    target_row = jnp.transpose(target)[:1, :]
    wanted = lax.broadcasted_iota(jnp.int32, (slots, rows), 0).astype(f32)
    select = jnp.where(wanted == target_row, 1.0, 0.0).astype(bf16)
    slot_gate = jnp.dot(
        select,
        jnp.broadcast_to(gate, (rows, LANES)).astype(bf16),
        preferred_element_type=f32,
    )[:, :1]

    for place in range(slabs):
        cols = slice(place * wide, (place + 1) * wide)
        both = []
        for kind in range(2):
            p = kind * slabs + place
            total = base_ref[kind, :, cols] + times_piece(x_ref, held_ref, p, copies[p])
            if kind == 0:
                acc_ref[:, cols] = total
            both.append(total)
        gated = acc_ref[:, cols] * inverse
        act = (gated / (1.0 + jnp.exp(-gated)) * (both[1] * inverse)).astype(bf16)
        act_ref[:, cols] = jnp.dot(select, act, preferred_element_type=f32).astype(bf16)

    out_copies = []
    for j, group in enumerate(down_copies):
        cols = slice(j * tile, (j + 1) * tile)
        for copy in group:
            copy.wait()
        total = jnp.dot(act_ref[...], down_ref[:, cols], preferred_element_type=f32)
        out_ref[:, cols] = (total * slot_gate).astype(bf16)
        copy = pltpu.make_async_copy(out_ref.at[:, cols], out_hbm.at[:, cols], out_sems.at[j])
        copy.start()
        out_copies.append(copy)
    for copy in out_copies:
        copy.wait()


def in_vmem():
    return pl.BlockSpec(memory_space=pltpu.VMEM)


def in_any():
    return pl.BlockSpec(memory_space=pl.ANY)


def gate_up(a, b, gates, ups):
    half, columns = a[0].shape
    rows = 2 * half
    pieces = gates + ups
    wide = pieces[0].shape[2]
    hidden = wide * len(gates)
    return pl.pallas_call(
        functools.partial(gate_up_kernel, len(gates), rows // 4, columns),
        in_specs=[in_vmem()] * 4 + [in_any()] * len(pieces),
        out_specs=in_vmem(),
        out_shape=jax.ShapeDtypeStruct((2, rows, hidden), f32),
        scratch_shapes=[
            pltpu.VMEM((rows, 2 * columns), bf16),
            pltpu.VMEM((len(pieces), 2 * columns, wide), bf16),
            pltpu.SemaphoreType.DMA((len(pieces) + 1,)),
        ],
        compiler_params=pltpu.CompilerParams(vmem_limit_bytes=20 << 20),
        cost_estimate=pl.CostEstimate(
            flops=8 * rows * columns * hidden,
            bytes_accessed=8 * columns * hidden + 8 * rows * hidden,
            transcendentals=0,
        ),
        name="gate_up",
    )(*a, *b, *map(in_hbm, pieces))


def finish(place, a, b, base, gates, ups, downs, block, order, top, senders, capacity):
    half, columns = a[0].shape
    rows = 2 * half
    pieces = gates + ups
    wide = pieces[0].shape[2]
    hidden = wide * len(gates)
    width = downs[0].shape[2]
    tiles = width // column_tile(width, 1024)
    slots = senders * capacity
    return pl.pallas_call(
        functools.partial(
            finish_kernel, len(gates), rows // 4, columns, block, order, top, senders
        ),
        in_specs=[pl.BlockSpec(memory_space=pltpu.SMEM)]
        + [in_vmem()] * 5
        + [in_any()] * (len(pieces) + len(downs)),
        out_specs=in_any(),
        out_shape=jax.ShapeDtypeStruct((slots, width), bf16),
        scratch_shapes=[
            pltpu.VMEM((rows, 2 * columns), bf16),
            pltpu.VMEM((len(pieces), 2 * columns, wide), bf16),
            pltpu.VMEM((rows, hidden), f32),
            pltpu.VMEM((slots, hidden), bf16),
            pltpu.VMEM((hidden, width), bf16),
            pltpu.VMEM((slots, width), bf16),
            pltpu.SemaphoreType.DMA((len(pieces) + 1,)),
            pltpu.SemaphoreType.DMA((tiles, len(downs))),
            pltpu.SemaphoreType.DMA((tiles,)),
        ],
        compiler_params=pltpu.CompilerParams(vmem_limit_bytes=42 << 20),
        cost_estimate=pl.CostEstimate(
            flops=8 * rows * columns * hidden + 2 * slots * hidden * width,
            bytes_accessed=8 * columns * hidden + 2 * hidden * width + 2 * slots * width,
            transcendentals=rows * hidden,
        ),
        name="finish",
    )(place, *a, *b, base, *map(in_hbm, pieces + downs))


def add(a, b):
    return (a.astype(f32) + b.astype(f32)).astype(bf16)


def swap(value, bit, count):
    return lax.ppermute(value, "exp", [(i, i ^ (1 << bit)) for i in range(count)])


def shifted(value, count):
    return [value] + [
        lax.ppermute(value, "ctx", [(i, (i + k) % count) for i in range(count)])
        for k in range(1, count)
    ]


def tie(*values):
    return lax.optimization_barrier(values)


def first_swap(parts, count):
    _, send_a, _, send_b = parts
    return swap(send_a, 0, count), swap(send_b, 1, count)


def second_swap(parts, got, count):
    keep_a, _, keep_b, _ = parts
    got_a, got_b = got
    half = keep_a.shape[0] // 2
    next_a = add(keep_a[half:], got_a[half:])
    next_b = add(keep_b[half:], got_b[half:])
    got_a2, got_b2 = swap(next_a, 1, count), swap(next_b, 0, count)
    keep_a = add(keep_a[:half], got_a[:half])
    keep_b = add(keep_b[:half], got_b[:half])
    return keep_a, keep_b, got_a2, got_b2


def last_swaps(terms, count, bits):
    keep_a, keep_b, got_a, got_b = terms
    keep = jnp.concatenate([keep_a, keep_b], axis=1)
    got = jnp.concatenate([got_a, got_b], axis=1)
    for bit in range(2, bits):
        half = keep.shape[0] // 2
        arrived = swap(add(keep[half:], got[half:]), bit, count)
        keep, got = add(keep[:half], got[:half]), arrived
    return keep, got


def gather_rows(rows, split, count, bits):
    for bit in range(bits - 1, 1, -1):
        rows = jnp.concatenate([rows, swap(rows, bit, count)], axis=0)
    out = []
    for part, (first, second) in ((rows[:, :split], (1, 0)), (rows[:, split:], (0, 1))):
        low = jnp.concatenate([part, swap(part, first, count)], axis=0)
        out.append([low, swap(low, second, count)])
    return out


def body(
    queries, latent, value_up, out_proj, residual, norm_gain, routes, gates, w_gate, w_up, w_down
):
    slabs = lax.axis_size("ctx")
    senders = lax.axis_size("exp")
    bits = bits_of(senders)
    block, width = residual.shape
    top = routes.shape[1]
    expert_count = senders * w_gate.shape[0]
    capacity = max(2, 3 * block * top // (2 * expert_count))
    orders = (list(range(bits)), [1, 0, *range(2, bits)])
    place = jnp.stack([lax.axis_index("ctx"), lax.axis_index("exp")]).astype(jnp.int32)

    keys = shifted(latent.T, slabs)
    arrived, gate_source, up_source = tie(keys[1:], w_gate, w_up)
    keys = [keys[0], *arrived]
    gate_others = shifted(gate_source, slabs)[1:]
    up_others = shifted(up_source, slabs)[1:]

    hva, hvb, *parts = attend_project(
        place, queries, keys, value_up, out_proj, block, orders
    )
    more = project_more(hva, hvb, out_proj, 1)
    got = first_swap(parts, senders)
    got, more, gate_others = tie(got, more, gate_others)
    terms = [second_swap(parts, got, senders)]
    got = first_swap(more, senders)
    got, terms[0], up_others, down_source = tie(got, terms[0], up_others, w_down)
    down_others = shifted(down_source, slabs)[1:]
    terms.append(second_swap(more, got, senders))
    sums = [last_swaps(t, senders, bits) for t in terms]
    sums[1], down_others = tie(sums[1], down_others)
    gate_parts = [w_gate, *gate_others]
    up_parts = [w_up, *up_others]
    down_parts = [w_down, *down_others]
    half_width = width // 2
    gain = norm_gain.astype(f32)
    hidden, payload, squares = [], [], 0.0
    for c, (keep, got) in enumerate(sums):
        cols = slice(c * half_width, (c + 1) * half_width)
        rows = (residual[:, cols].astype(f32) + (keep.astype(f32) + got.astype(f32))).astype(bf16)
        wide = rows.astype(f32)
        squares = squares + jnp.sum(wide * wide, axis=1, keepdims=True)
        hidden.append(rows)
        payload.append((wide * gain[None, cols]).astype(bf16))
    inverse = lax.rsqrt(squares / width + norm_epsilon)
    coarse = lax.reduce_precision(inverse, 8, 7)
    meta = jnp.concatenate(
        [
            routes.astype(bf16),
            gates.astype(bf16),
            coarse.astype(bf16),
            (inverse - coarse).astype(bf16),
            jnp.zeros((block, LANES - 2 * top - 2), bf16),
        ],
        axis=1,
    )
    payload[1] = jnp.concatenate([payload[1], meta], axis=1)

    a, b = gather_rows(payload[0], half_width // 2, senders, bits)
    base = gate_up(a, b, gate_parts, up_parts)
    a, b = gather_rows(payload[1], half_width // 2, senders, bits)
    slots = finish(
        place, a, b, base, gate_parts, up_parts, down_parts, block, orders[0], top, senders, capacity
    )
    expert_out = slots.reshape(capacity, senders, width).transpose(1, 0, 2)[None, None]
    return jnp.concatenate(hidden, axis=1), expert_out


def solution(mesh):
    placed = (
        P("ctx", "exp"),
        P("ctx", None),
        P("exp", None, None),
        P("exp", None),
        P(("ctx", "exp"), None),
        P(),
        P(("ctx", "exp"), None),
        P(("ctx", "exp"), None),
        P("exp", None, "ctx"),
        P("exp", None, "ctx"),
        P("exp", "ctx", None),
    )
    return jax.shard_map(
        body,
        mesh=mesh,
        in_specs=placed,
        out_specs=(P(("ctx", "exp"), None), P("ctx", "exp", None, None, None)),
        check_vma=False,
    )
```

```python
import functools
import math

import jax
import jax.numpy as jnp
from jax import lax
from jax.experimental import pallas as pl
from jax.experimental.pallas import tpu as pltpu
from jax.sharding import PartitionSpec as P

score_scale = 192.0 ** (-0.5)
norm_epsilon = 1e-06
masked_value = -1e30
LANES = 128
first_share = 12
f32 = jnp.float32
bf16 = jnp.bfloat16


def bits_of(count):
    return count.bit_length() - 1


def relative_of(pos, order):
    rel = jnp.zeros_like(pos)
    for i, bit in enumerate(order):
        rel = rel | (((pos >> (len(order) - 1 - i)) & 1) << bit)
    return rel


def order_matrix(rows, block, order, me):
    shift = bits_of(block)
    row = lax.broadcasted_iota(jnp.int32, (rows, rows), 0)
    col = lax.broadcasted_iota(jnp.int32, (rows, rows), 1)
    source = ((relative_of(row >> shift, order) ^ me) << shift) | (row & (block - 1))
    return jnp.where(col == source, 1.0, 0.0).astype(bf16)


def attend_kernel(
    slabs, block, orders, place_ref, q_ref, *refs
):
    keys = refs[:slabs]
    up_ref, wa_ref, wb_ref = refs[slabs : slabs + 3]
    hva_ref, hvb_ref, ka_ref, sa_ref, kb_ref, sb_ref = refs[slabs + 3 : slabs + 9]
    padded_ref, hv_ref = refs[slabs + 9 :]
    heads, latent_width, value_width = up_ref.shape
    qk, slab = keys[0].shape
    rows = q_ref.shape[0]
    span = slab * slabs

    @pl.when(pl.program_id(0) == 0)
    def _():
        here = place_ref[0]
        me = place_ref[1]
        offsets = sorted({(h * qk) % LANES for h in range(heads)})
        padded_ref[...] = jnp.zeros_like(padded_ref)
        for n, offset in enumerate(offsets):
            for k in range(slabs):
                padded_ref[n, offset : offset + qk, k * slab : (k + 1) * slab] = keys[k][...]
        col = lax.broadcasted_iota(jnp.int32, (rows, span), 1)
        key_pos = col
        for k in range(slabs):
            base = lax.rem(here - k + slabs, slabs) * slab
            key_pos = jnp.where(col >= k * slab, col - k * slab + base, key_pos)
        query_pos = lax.broadcasted_iota(jnp.int32, (rows, span), 0) + here * slab
        visible = (key_pos <= query_pos) & (key_pos > query_pos - span // 2)
        for h in range(heads):
            offset = (h * qk) % LANES
            start = h * qk - offset
            width = -(-(offset + qk) // LANES) * LANES
            n = offsets.index(offset)
            scores = (
                jnp.dot(
                    q_ref[:, start : start + width],
                    padded_ref[n, :width, :],
                    preferred_element_type=f32,
                )
                * score_scale
            )
            masked = jnp.where(visible, scores, masked_value)
            top = jnp.max(masked, axis=1, keepdims=True)
            weights = jnp.where(visible, jnp.exp(masked - top), 0.0)
            total = jnp.sum(weights, axis=1, keepdims=True)
            mixed = lax.dot_general(
                weights.astype(bf16),
                padded_ref[0, :latent_width, :],
                (((1,), (1,)), ((), ())),
                preferred_element_type=f32,
            )
            attended = (mixed / total).astype(bf16)
            hv_ref[:, h * value_width : (h + 1) * value_width] = jnp.dot(
                attended, up_ref[h], preferred_element_type=f32
            ).astype(bf16)
        hv = hv_ref[...]
        for out_ref, order in zip((hva_ref, hvb_ref), orders):
            out_ref[...] = jnp.dot(
                order_matrix(rows, block, order, me), hv, preferred_element_type=f32
            ).astype(bf16)

    project(hva_ref, wa_ref, ka_ref, sa_ref)
    project(hvb_ref, wb_ref, kb_ref, sb_ref)


def project(hv_ref, w_ref, keep_ref, send_ref):
    half = keep_ref.shape[0]
    out = jnp.dot(hv_ref[...], w_ref[...], preferred_element_type=f32).astype(bf16)
    keep_ref[...] = out[:half]
    send_ref[...] = out[half:]


def project_kernel(hva_ref, hvb_ref, wa_ref, wb_ref, ka_ref, sa_ref, kb_ref, sb_ref):
    project(hva_ref, wa_ref, ka_ref, sa_ref)
    project(hvb_ref, wb_ref, kb_ref, sb_ref)


def in_hbm(value):
    return pltpu.with_memory_space_constraint(value, pltpu.HBM)


def column_tile(columns, most):
    tiles = columns // LANES
    return LANES * max(t for t in range(1, tiles + 1) if tiles % t == 0 and t * LANES <= most)


def project_specs(rows, inner, first, half):
    tile = column_tile(math.gcd(first, half), 1024)
    steps = half // tile
    weights = [
        pl.BlockSpec((inner, tile), lambda i, at=at: (0, at + i))
        for at in (first // tile, first // tile + steps)
    ]
    outs = [pl.BlockSpec((rows // 2, tile), lambda i: (0, i))] * 4
    shapes = [jax.ShapeDtypeStruct((rows // 2, half), bf16)] * 4
    return steps, weights, outs, shapes


def whole(shape):
    return pl.BlockSpec(shape, lambda i: (0,) * len(shape))


def attend_project(place, queries, keys, value_up, out_proj, half, block, orders):
    rows, _ = queries.shape
    heads, _, value_width = value_up.shape
    qk, slab = keys[0].shape
    slabs = len(keys)
    span = slab * slabs
    inner = out_proj.shape[0]
    steps, weights, outs, shapes = project_specs(rows, inner, 0, half)
    offsets = {(h * qk) % LANES for h in range(heads)}
    deep = max(-(-(o + qk) // LANES) * LANES for o in offsets)
    flops = 2 * rows * (heads * span * 2 * qk + inner * 2 * half)
    return pl.pallas_call(
        functools.partial(attend_kernel, slabs, block, orders),
        grid=(steps,),
        in_specs=[
            pl.BlockSpec(memory_space=pltpu.SMEM),
            whole(queries.shape),
            *[whole(k.shape) for k in keys],
            whole(value_up.shape),
            *weights,
        ],
        out_specs=[whole((rows, inner))] * 2 + outs,
        out_shape=[jax.ShapeDtypeStruct((rows, inner), bf16)] * 2 + shapes,
        scratch_shapes=[
            pltpu.VMEM((len(offsets), deep, span), bf16),
            pltpu.VMEM((rows, inner), bf16),
        ],
        compiler_params=pltpu.CompilerParams(vmem_limit_bytes=24 << 20),
        cost_estimate=pl.CostEstimate(
            flops=flops,
            bytes_accessed=4 * (inner + rows) * half + queries.size * 2,
            transcendentals=rows * span * heads,
        ),
        name="attend_project",
    )(place, in_hbm(queries), in_hbm(keys[0]), *keys[1:], in_hbm(value_up), in_hbm(out_proj), in_hbm(out_proj))


def project_more(hva, hvb, out_proj, first, half):
    rows, inner = hva.shape
    steps, weights, outs, shapes = project_specs(rows, inner, first, half)
    return pl.pallas_call(
        project_kernel,
        grid=(steps,),
        in_specs=[whole(hva.shape), whole(hvb.shape), *weights],
        out_specs=outs,
        out_shape=shapes,
        compiler_params=pltpu.CompilerParams(vmem_limit_bytes=16 << 20),
        cost_estimate=pl.CostEstimate(
            flops=4 * rows * inner * half,
            bytes_accessed=4 * (inner + rows) * half,
            transcendentals=0,
        ),
        name="project_more",
    )(hva, hvb, in_hbm(out_proj), in_hbm(out_proj))


def place_rows(quarter_rows, columns, a_refs, b_refs, x_ref):
    a_low, a_high = a_refs
    b_low, b_high = b_refs
    q = quarter_rows
    for ref, source, count, target, first in (
        (a_low, 0, 2 * q, 0, 0),
        (a_high, 0, 2 * q, 2 * q, 0),
        (b_low, 0, q, 0, columns),
        (b_low, q, q, 2 * q, columns),
        (b_high, 0, q, q, columns),
        (b_high, q, q, 3 * q, columns),
    ):
        x_ref[target : target + count, first : first + columns] = ref[
            source : source + count, :columns
        ]


def weight_copies(pieces, held_ref, sems, first_row):
    deep = held_ref.shape[1]
    copies = []
    for p, w_ref in enumerate(pieces):
        cuts = (0, deep // 2, deep) if p == 0 else (0, deep)
        for n, (low, high) in enumerate(zip(cuts, cuts[1:])):
            copy = pltpu.make_async_copy(
                w_ref.at[0, first_row + low : first_row + high, :],
                held_ref.at[p, low:high, :],
                sems.at[p + (n if p == 0 else 1)],
            )
            copies.append((p, low, high, [copy]))
    return copies


class Window:
    def __init__(self, groups, ahead):
        self.groups, self.ahead, self.used = groups, ahead, 0
        for group in groups[:ahead]:
            self.start(group)

    def start(self, group):
        for copy in group:
            copy.start()

    def take(self):
        for copy in self.groups[self.used]:
            copy.wait()
        if self.used + self.ahead < len(self.groups):
            self.start(self.groups[self.used + self.ahead])
        self.used += 1


def times_piece(x_ref, held_ref, window, copies, piece):
    total = None
    for p, low, high, _ in copies:
        if p == piece:
            window.take()
            term = jnp.dot(x_ref[:, low:high], held_ref[p, low:high, :], preferred_element_type=f32)
            total = term if total is None else total + term
    return total


def gate_up_kernel(slabs, quarter_rows, columns, *refs):
    a_refs, b_refs = refs[:2], refs[2:4]
    pieces = refs[4 : 4 + 2 * slabs]
    acc_ref, x_ref, held_ref, sems = refs[4 + 2 * slabs :]
    copies = weight_copies(pieces, held_ref, sems, 0)
    window = Window([c[3] for c in copies], 3)
    place_rows(quarter_rows, columns, a_refs, b_refs, x_ref)
    wide = held_ref.shape[2]
    for p in range(len(pieces)):
        place, kind = divmod(p, 2)
        acc_ref[kind, :, place * wide : (place + 1) * wide] = times_piece(
            x_ref, held_ref, window, copies, p
        )


def finish_kernel(slabs, quarter_rows, columns, first_row, block, order, top, senders, place_ref, *refs):
    a_refs, b_refs = refs[:2], refs[2:4]
    base_ref = refs[4]
    pieces = refs[5 : 5 + 2 * slabs]
    downs = refs[5 + 2 * slabs : 5 + 3 * slabs]
    (out_hbm, x_ref, held_ref, acc_ref, act_ref, down_ref, out_ref, sems, down_sems, out_sems) = refs[
        5 + 3 * slabs :
    ]
    rows = 4 * quarter_rows
    q = quarter_rows
    slots, width = out_ref.shape
    part = downs[0].shape[1]
    wide = held_ref.shape[2]
    tiles = down_sems.shape[0]
    tile = width // tiles
    copies = weight_copies(pieces, held_ref, sems, first_row)
    down_copies = [
        [
            pltpu.make_async_copy(
                w_ref.at[0, :, j * tile : (j + 1) * tile],
                down_ref.at[p * part : (p + 1) * part, j * tile : (j + 1) * tile],
                down_sems.at[j, p],
            )
            for p, w_ref in enumerate(downs)
        ]
        for j in range(tiles)
    ]
    window = Window([c[3] for c in copies] + down_copies, 3)
    place_rows(quarter_rows, columns, a_refs, b_refs, x_ref)

    me = place_ref[1]
    b_low, b_high = b_refs
    meta = jnp.concatenate(
        [b_low[:q, columns:], b_high[:q, columns:], b_low[q:, columns:], b_high[q:, columns:]],
        axis=0,
    ).astype(f32)
    lane = lax.broadcasted_iota(jnp.int32, (rows, LANES), 1)
    named = (lane < top) & (meta == me.astype(f32))
    hit = jnp.max(jnp.where(named, 1.0, 0.0), axis=1, keepdims=True)
    aligned = pltpu.roll(meta, LANES - top, 1)
    gate = jnp.sum(jnp.where(named, aligned, 0.0), axis=1, keepdims=True)
    inverse = jnp.sum(
        jnp.where((lane == 2 * top) | (lane == 2 * top + 1), meta, 0.0), axis=1, keepdims=True
    )
    r = lax.broadcasted_iota(jnp.int32, (rows, rows), 0)
    c = lax.broadcasted_iota(jnp.int32, (rows, rows), 1)
    shift = bits_of(block)
    before = jnp.where(((r >> shift) == (c >> shift)) & (c < r), 1.0, 0.0).astype(bf16)
    hits = jnp.broadcast_to(hit, (rows, LANES))
    slot = jnp.dot(before, hits.astype(bf16), preferred_element_type=f32)
    pos = lax.broadcasted_iota(jnp.int32, (rows, LANES), 0) >> shift
    sender = (relative_of(pos, order) ^ me).astype(f32)
    target = jnp.where(hits > 0.5, slot * senders + sender, -1.0)
    target_row = jnp.transpose(target)[:1, :]
    wanted = lax.broadcasted_iota(jnp.int32, (slots, rows), 0).astype(f32)
    select = jnp.where(wanted == target_row, 1.0, 0.0).astype(bf16)
    slot_gate = jnp.dot(
        select,
        jnp.broadcast_to(gate, (rows, LANES)).astype(bf16),
        preferred_element_type=f32,
    )[:, :1]

    for place in range(slabs):
        cols = slice(place * wide, (place + 1) * wide)
        both = []
        for kind in range(2):
            total = base_ref[kind, :, cols] + times_piece(
                x_ref, held_ref, window, copies, 2 * place + kind
            )
            if kind == 0:
                acc_ref[:, cols] = total
            both.append(total)
        gated = acc_ref[:, cols] * inverse
        act = (gated / (1.0 + jnp.exp(-gated)) * (both[1] * inverse)).astype(bf16)
        act_ref[:, cols] = jnp.dot(select, act, preferred_element_type=f32).astype(bf16)

    out_copies = []
    for j in range(tiles):
        cols = slice(j * tile, (j + 1) * tile)
        window.take()
        total = jnp.dot(act_ref[...], down_ref[:, cols], preferred_element_type=f32)
        out_ref[:, cols] = (total * slot_gate).astype(bf16)
        copy = pltpu.make_async_copy(out_ref.at[:, cols], out_hbm.at[:, cols], out_sems.at[j])
        copy.start()
        out_copies.append(copy)
    for copy in out_copies:
        copy.wait()


def in_vmem():
    return pl.BlockSpec(memory_space=pltpu.VMEM)


def in_any():
    return pl.BlockSpec(memory_space=pl.ANY)


def gate_up(a, b, gates, ups):
    half, columns = a[0].shape
    rows = 2 * half
    pieces = [w for pair in zip(gates, ups) for w in pair]
    wide = pieces[0].shape[2]
    hidden = wide * len(gates)
    return pl.pallas_call(
        functools.partial(gate_up_kernel, len(gates), rows // 4, columns),
        in_specs=[in_vmem()] * 4 + [in_any()] * len(pieces),
        out_specs=in_vmem(),
        out_shape=jax.ShapeDtypeStruct((2, rows, hidden), f32),
        scratch_shapes=[
            pltpu.VMEM((rows, 2 * columns), bf16),
            pltpu.VMEM((len(pieces), 2 * columns, wide), bf16),
            pltpu.SemaphoreType.DMA((len(pieces) + 1,)),
        ],
        compiler_params=pltpu.CompilerParams(vmem_limit_bytes=20 << 20),
        cost_estimate=pl.CostEstimate(
            flops=8 * rows * columns * hidden,
            bytes_accessed=8 * columns * hidden + 8 * rows * hidden,
            transcendentals=0,
        ),
        name="gate_up",
    )(*a, *b, *map(in_hbm, pieces))


def finish(place, a, b, base, gates, ups, downs, first_row, block, order, top, senders, capacity):
    half, columns = a[0].shape
    rows = 2 * half
    pieces = [w for pair in zip(gates, ups) for w in pair]
    wide = pieces[0].shape[2]
    hidden = wide * len(gates)
    width = downs[0].shape[2]
    tiles = width // column_tile(width, 1024)
    slots = senders * capacity
    return pl.pallas_call(
        functools.partial(
            finish_kernel, len(gates), rows // 4, columns, first_row, block, order, top, senders
        ),
        in_specs=[pl.BlockSpec(memory_space=pltpu.SMEM)]
        + [in_vmem()] * 5
        + [in_any()] * (len(pieces) + len(downs)),
        out_specs=in_any(),
        out_shape=jax.ShapeDtypeStruct((slots, width), bf16),
        scratch_shapes=[
            pltpu.VMEM((rows, 2 * columns), bf16),
            pltpu.VMEM((len(pieces), 2 * columns, wide), bf16),
            pltpu.VMEM((rows, hidden), f32),
            pltpu.VMEM((slots, hidden), bf16),
            pltpu.VMEM((hidden, width), bf16),
            pltpu.VMEM((slots, width), bf16),
            pltpu.SemaphoreType.DMA((len(pieces) + 1,)),
            pltpu.SemaphoreType.DMA((tiles, len(downs))),
            pltpu.SemaphoreType.DMA((tiles,)),
        ],
        compiler_params=pltpu.CompilerParams(vmem_limit_bytes=42 << 20),
        cost_estimate=pl.CostEstimate(
            flops=8 * rows * columns * hidden + 2 * slots * hidden * width,
            bytes_accessed=8 * columns * hidden + 2 * hidden * width + 2 * slots * width,
            transcendentals=rows * hidden,
        ),
        name="finish",
    )(place, *a, *b, base, *map(in_hbm, pieces + downs))


def add(a, b):
    return (a.astype(f32) + b.astype(f32)).astype(bf16)


def swap(value, bit, count):
    return lax.ppermute(value, "exp", [(i, i ^ (1 << bit)) for i in range(count)])


def shifted(value, count):
    return [value] + [
        lax.ppermute(value, "ctx", [(i, (i + k) % count) for i in range(count)])
        for k in range(1, count)
    ]


def tie(*values):
    return lax.optimization_barrier(values)


def first_swap(parts, count):
    _, send_a, _, send_b = parts
    return swap(send_a, 0, count), swap(send_b, 1, count)


def second_swap(parts, got, count):
    keep_a, _, keep_b, _ = parts
    got_a, got_b = got
    half = keep_a.shape[0] // 2
    next_a = add(keep_a[half:], got_a[half:])
    next_b = add(keep_b[half:], got_b[half:])
    got_a2, got_b2 = swap(next_a, 1, count), swap(next_b, 0, count)
    keep_a = add(keep_a[:half], got_a[:half])
    keep_b = add(keep_b[:half], got_b[:half])
    return keep_a, keep_b, got_a2, got_b2


def last_swaps(terms, count, bits):
    keep_a, keep_b, got_a, got_b = terms
    keep = jnp.concatenate([keep_a, keep_b], axis=1)
    got = jnp.concatenate([got_a, got_b], axis=1)
    for bit in range(2, bits):
        half = keep.shape[0] // 2
        arrived = swap(add(keep[half:], got[half:]), bit, count)
        keep, got = add(keep[:half], got[:half]), arrived
    return keep, got


def gather_rows(rows, split, count, bits):
    for bit in range(bits - 1, 1, -1):
        rows = jnp.concatenate([rows, swap(rows, bit, count)], axis=0)
    out = []
    for part, (first, second) in ((rows[:, :split], (1, 0)), (rows[:, split:], (0, 1))):
        low = jnp.concatenate([part, swap(part, first, count)], axis=0)
        out.append([low, swap(low, second, count)])
    return out


def body(
    queries, latent, value_up, out_proj, residual, norm_gain, routes, gates, w_gate, w_up, w_down
):
    slabs = lax.axis_size("ctx")
    senders = lax.axis_size("exp")
    bits = bits_of(senders)
    block, width = residual.shape
    top = routes.shape[1]
    expert_count = senders * w_gate.shape[0]
    capacity = max(2, 3 * block * top // (2 * expert_count))
    orders = (list(range(bits)), [1, 0, *range(2, bits)])
    tiles = width // (2 * LANES)
    low = LANES * (tiles * first_share // 28)
    halves = (low, LANES * tiles - low)
    place = jnp.stack([lax.axis_index("ctx"), lax.axis_index("exp")]).astype(jnp.int32)

    keys = shifted(latent.T, slabs)
    arrived, gate_source, up_source = tie(keys[1:], w_gate, w_up)
    keys = [keys[0], *arrived]
    gate_others = shifted(gate_source, slabs)[1:]
    up_others = shifted(up_source, slabs)[1:]

    hva, hvb, *parts = attend_project(
        place, queries, keys, value_up, out_proj, halves[0], block, orders
    )
    more = project_more(hva, hvb, out_proj, 2 * halves[0], halves[1])
    got = first_swap(parts, senders)
    got, more, gate_others = tie(got, more, gate_others)
    terms = [second_swap(parts, got, senders)]
    got = first_swap(more, senders)
    got, terms[0], up_others, down_source = tie(got, terms[0], up_others, w_down)
    down_others = shifted(down_source, slabs)[1:]
    terms.append(second_swap(more, got, senders))
    sums = [last_swaps(t, senders, bits) for t in terms]
    sums[1], down_others = tie(sums[1], down_others)
    gate_parts = [w_gate, *gate_others]
    up_parts = [w_up, *up_others]
    down_parts = [w_down, *down_others]
    gain = norm_gain.astype(f32)
    hidden, payload, squares = [], [], 0.0
    for c, (keep, got) in enumerate(sums):
        cols = slice(2 * halves[0] * c, 2 * (halves[0] + halves[1] * c))
        rows = (residual[:, cols].astype(f32) + (keep.astype(f32) + got.astype(f32))).astype(bf16)
        wide = rows.astype(f32)
        squares = squares + jnp.sum(wide * wide, axis=1, keepdims=True)
        hidden.append(rows)
        payload.append((wide * gain[None, cols]).astype(bf16))
    inverse = lax.rsqrt(squares / width + norm_epsilon)
    coarse = lax.reduce_precision(inverse, 8, 7)
    meta = jnp.concatenate(
        [
            routes.astype(bf16),
            gates.astype(bf16),
            coarse.astype(bf16),
            (inverse - coarse).astype(bf16),
            jnp.zeros((block, LANES - 2 * top - 2), bf16),
        ],
        axis=1,
    )
    payload[1] = jnp.concatenate([payload[1], meta], axis=1)

    a, b = gather_rows(payload[0], halves[0], senders, bits)
    base = gate_up(a, b, gate_parts, up_parts)
    a, b = gather_rows(payload[1], halves[1], senders, bits)
    slots = finish(
        place, a, b, base, gate_parts, up_parts, down_parts, 2 * halves[0], block, orders[0], top, senders, capacity
    )
    expert_out = slots.reshape(capacity, senders, width).transpose(1, 0, 2)[None, None]
    return jnp.concatenate(hidden, axis=1), expert_out


def solution(mesh):
    placed = (
        P("ctx", "exp"),
        P("ctx", None),
        P("exp", None, None),
        P("exp", None),
        P(("ctx", "exp"), None),
        P(),
        P(("ctx", "exp"), None),
        P(("ctx", "exp"), None),
        P("exp", None, "ctx"),
        P("exp", None, "ctx"),
        P("exp", "ctx", None),
    )
    return jax.shard_map(
        body,
        mesh=mesh,
        in_specs=placed,
        out_specs=(P(("ctx", "exp"), None), P("ctx", "exp", None, None, None)),
        check_vma=False,
    )
```

```python
import functools
import math

import jax
import jax.numpy as jnp
from jax import lax
from jax.experimental import pallas as pl
from jax.experimental.pallas import tpu as pltpu
from jax.sharding import PartitionSpec as P

score_scale = 192.0 ** (-0.5)
norm_epsilon = 1e-06
masked_value = -1e30
LANES = 128
first_share = 16
f32 = jnp.float32
bf16 = jnp.bfloat16


def bits_of(count):
    return count.bit_length() - 1


def relative_of(pos, order):
    rel = jnp.zeros_like(pos)
    for i, bit in enumerate(order):
        rel = rel | (((pos >> (len(order) - 1 - i)) & 1) << bit)
    return rel


def order_matrix(rows, block, order, me):
    shift = bits_of(block)
    row = lax.broadcasted_iota(jnp.int32, (rows, rows), 0)
    col = lax.broadcasted_iota(jnp.int32, (rows, rows), 1)
    source = ((relative_of(row >> shift, order) ^ me) << shift) | (row & (block - 1))
    return jnp.where(col == source, 1.0, 0.0).astype(bf16)


def attend_kernel(
    slabs, block, orders, place_ref, q_ref, *refs
):
    keys = refs[:slabs]
    up_ref, wa_ref, wb_ref = refs[slabs : slabs + 3]
    hva_ref, hvb_ref, ka_ref, sa_ref, kb_ref, sb_ref = refs[slabs + 3 : slabs + 9]
    padded_ref, hv_ref = refs[slabs + 9 :]
    heads, latent_width, value_width = up_ref.shape
    qk, slab = keys[0].shape
    rows = q_ref.shape[0]
    span = slab * slabs

    @pl.when(pl.program_id(0) == 0)
    def _():
        here = place_ref[0]
        me = place_ref[1]
        offsets = sorted({(h * qk) % LANES for h in range(heads)})
        padded_ref[...] = jnp.zeros_like(padded_ref)
        for n, offset in enumerate(offsets):
            for k in range(slabs):
                padded_ref[n, offset : offset + qk, k * slab : (k + 1) * slab] = keys[k][...]
        col = lax.broadcasted_iota(jnp.int32, (rows, span), 1)
        key_pos = col
        for k in range(slabs):
            base = lax.rem(here - k + slabs, slabs) * slab
            key_pos = jnp.where(col >= k * slab, col - k * slab + base, key_pos)
        query_pos = lax.broadcasted_iota(jnp.int32, (rows, span), 0) + here * slab
        visible = (key_pos <= query_pos) & (key_pos > query_pos - span // 2)
        for h in range(heads):
            offset = (h * qk) % LANES
            start = h * qk - offset
            width = -(-(offset + qk) // LANES) * LANES
            n = offsets.index(offset)
            scores = (
                jnp.dot(
                    q_ref[:, start : start + width],
                    padded_ref[n, :width, :],
                    preferred_element_type=f32,
                )
                * score_scale
            )
            masked = jnp.where(visible, scores, masked_value)
            top = jnp.max(masked, axis=1, keepdims=True)
            weights = jnp.where(visible, jnp.exp(masked - top), 0.0)
            total = jnp.sum(weights, axis=1, keepdims=True)
            mixed = lax.dot_general(
                weights.astype(bf16),
                padded_ref[0, :latent_width, :],
                (((1,), (1,)), ((), ())),
                preferred_element_type=f32,
            )
            attended = (mixed / total).astype(bf16)
            hv_ref[:, h * value_width : (h + 1) * value_width] = jnp.dot(
                attended, up_ref[h], preferred_element_type=f32
            ).astype(bf16)
        hv = hv_ref[...]
        for out_ref, order in zip((hva_ref, hvb_ref), orders):
            out_ref[...] = jnp.dot(
                order_matrix(rows, block, order, me), hv, preferred_element_type=f32
            ).astype(bf16)

    project(hva_ref, wa_ref, ka_ref, sa_ref)
    project(hvb_ref, wb_ref, kb_ref, sb_ref)


def project(hv_ref, w_ref, keep_ref, send_ref):
    half = keep_ref.shape[0]
    out = jnp.dot(hv_ref[...], w_ref[...], preferred_element_type=f32).astype(bf16)
    keep_ref[...] = out[:half]
    send_ref[...] = out[half:]


def project_kernel(hva_ref, hvb_ref, wa_ref, wb_ref, ka_ref, sa_ref, kb_ref, sb_ref):
    project(hva_ref, wa_ref, ka_ref, sa_ref)
    project(hvb_ref, wb_ref, kb_ref, sb_ref)


def in_hbm(value):
    return pltpu.with_memory_space_constraint(value, pltpu.HBM)


def column_tile(columns, most):
    tiles = columns // LANES
    return LANES * max(t for t in range(1, tiles + 1) if tiles % t == 0 and t * LANES <= most)


def project_specs(rows, inner, first, half):
    tile = column_tile(math.gcd(first, half), 1024)
    steps = half // tile
    weights = [
        pl.BlockSpec((inner, tile), lambda i, at=at: (0, at + i))
        for at in (first // tile, first // tile + steps)
    ]
    outs = [pl.BlockSpec((rows // 2, tile), lambda i: (0, i))] * 4
    shapes = [jax.ShapeDtypeStruct((rows // 2, half), bf16)] * 4
    return steps, weights, outs, shapes


def whole(shape):
    return pl.BlockSpec(shape, lambda i: (0,) * len(shape))


def attend_project(place, queries, keys, value_up, out_proj, half, block, orders):
    rows, _ = queries.shape
    heads, _, value_width = value_up.shape
    qk, slab = keys[0].shape
    slabs = len(keys)
    span = slab * slabs
    inner = out_proj.shape[0]
    steps, weights, outs, shapes = project_specs(rows, inner, 0, half)
    offsets = {(h * qk) % LANES for h in range(heads)}
    deep = max(-(-(o + qk) // LANES) * LANES for o in offsets)
    flops = 2 * rows * (heads * span * 2 * qk + inner * 2 * half)
    return pl.pallas_call(
        functools.partial(attend_kernel, slabs, block, orders),
        grid=(steps,),
        in_specs=[
            pl.BlockSpec(memory_space=pltpu.SMEM),
            whole(queries.shape),
            *[whole(k.shape) for k in keys],
            whole(value_up.shape),
            *weights,
        ],
        out_specs=[whole((rows, inner))] * 2 + outs,
        out_shape=[jax.ShapeDtypeStruct((rows, inner), bf16)] * 2 + shapes,
        scratch_shapes=[
            pltpu.VMEM((len(offsets), deep, span), bf16),
            pltpu.VMEM((rows, inner), bf16),
        ],
        compiler_params=pltpu.CompilerParams(vmem_limit_bytes=24 << 20),
        cost_estimate=pl.CostEstimate(
            flops=flops,
            bytes_accessed=4 * (inner + rows) * half + queries.size * 2,
            transcendentals=rows * span * heads,
        ),
        name="attend_project",
    )(place, in_hbm(queries), in_hbm(keys[0]), *keys[1:], in_hbm(value_up), in_hbm(out_proj), in_hbm(out_proj))


def project_more(hva, hvb, out_proj, first, half):
    rows, inner = hva.shape
    steps, weights, outs, shapes = project_specs(rows, inner, first, half)
    return pl.pallas_call(
        project_kernel,
        grid=(steps,),
        in_specs=[whole(hva.shape), whole(hvb.shape), *weights],
        out_specs=outs,
        out_shape=shapes,
        compiler_params=pltpu.CompilerParams(vmem_limit_bytes=16 << 20),
        cost_estimate=pl.CostEstimate(
            flops=4 * rows * inner * half,
            bytes_accessed=4 * (inner + rows) * half,
            transcendentals=0,
        ),
        name="project_more",
    )(hva, hvb, in_hbm(out_proj), in_hbm(out_proj))


def place_rows(quarter_rows, columns, a_refs, b_refs, x_ref):
    a_low, a_high = a_refs
    b_low, b_high = b_refs
    q = quarter_rows
    for ref, source, count, target, first in (
        (a_low, 0, 2 * q, 0, 0),
        (a_high, 0, 2 * q, 2 * q, 0),
        (b_low, 0, q, 0, columns),
        (b_low, q, q, 2 * q, columns),
        (b_high, 0, q, q, columns),
        (b_high, q, q, 3 * q, columns),
    ):
        x_ref[target : target + count, first : first + columns] = ref[
            source : source + count, :columns
        ]


def weight_copies(pieces, held_ref, sems, first_row):
    deep = held_ref.shape[1]
    copies = []
    for p, w_ref in enumerate(pieces):
        cuts = (0, deep // 2, deep) if p == 0 else (0, deep)
        for n, (low, high) in enumerate(zip(cuts, cuts[1:])):
            copy = pltpu.make_async_copy(
                w_ref.at[0, first_row + low : first_row + high, :],
                held_ref.at[p, low:high, :],
                sems.at[p + (n if p == 0 else 1)],
            )
            copies.append((p, low, high, [copy]))
    return copies


class Window:
    def __init__(self, groups, ahead):
        self.groups, self.ahead, self.used = groups, ahead, 0
        for group in groups[:ahead]:
            self.start(group)

    def start(self, group):
        for copy in group:
            copy.start()

    def take(self):
        for copy in self.groups[self.used]:
            copy.wait()
        if self.used + self.ahead < len(self.groups):
            self.start(self.groups[self.used + self.ahead])
        self.used += 1


def times_piece(x_ref, held_ref, window, copies, piece):
    total = None
    for p, low, high, _ in copies:
        if p == piece:
            window.take()
            term = jnp.dot(x_ref[:, low:high], held_ref[p, low:high, :], preferred_element_type=f32)
            total = term if total is None else total + term
    return total


def gate_up_kernel(slabs, quarter_rows, columns, *refs):
    a_refs, b_refs = refs[:2], refs[2:4]
    pieces = refs[4 : 4 + 2 * slabs]
    acc_ref, x_ref, held_ref, sems = refs[4 + 2 * slabs :]
    copies = weight_copies(pieces, held_ref, sems, 0)
    window = Window([c[3] for c in copies], 3)
    place_rows(quarter_rows, columns, a_refs, b_refs, x_ref)
    wide = held_ref.shape[2]
    for p in range(len(pieces)):
        place, kind = divmod(p, 2)
        acc_ref[kind, :, place * wide : (place + 1) * wide] = times_piece(
            x_ref, held_ref, window, copies, p
        )


def finish_kernel(slabs, quarter_rows, columns, first_row, block, order, top, senders, place_ref, *refs):
    a_refs, b_refs = refs[:2], refs[2:4]
    base_ref = refs[4]
    pieces = refs[5 : 5 + 2 * slabs]
    downs = refs[5 + 2 * slabs : 5 + 3 * slabs]
    (out_hbm, x_ref, held_ref, acc_ref, act_ref, down_ref, out_ref, sems, down_sems, out_sems) = refs[
        5 + 3 * slabs :
    ]
    rows = 4 * quarter_rows
    q = quarter_rows
    slots, width = out_ref.shape
    part = downs[0].shape[1]
    wide = held_ref.shape[2]
    tiles = down_sems.shape[0]
    tile = width // tiles
    copies = weight_copies(pieces, held_ref, sems, first_row)
    down_copies = [
        [
            pltpu.make_async_copy(
                w_ref.at[0, :, j * tile : (j + 1) * tile],
                down_ref.at[p * part : (p + 1) * part, j * tile : (j + 1) * tile],
                down_sems.at[j, p],
            )
            for p, w_ref in enumerate(downs)
        ]
        for j in range(tiles)
    ]
    window = Window([c[3] for c in copies] + down_copies, 3)
    place_rows(quarter_rows, columns, a_refs, b_refs, x_ref)

    me = place_ref[1]
    b_low, b_high = b_refs
    meta = jnp.concatenate(
        [b_low[:q, columns:], b_high[:q, columns:], b_low[q:, columns:], b_high[q:, columns:]],
        axis=0,
    ).astype(f32)
    lane = lax.broadcasted_iota(jnp.int32, (rows, LANES), 1)
    named = (lane < top) & (meta == me.astype(f32))
    hit = jnp.max(jnp.where(named, 1.0, 0.0), axis=1, keepdims=True)
    aligned = pltpu.roll(meta, LANES - top, 1)
    gate = jnp.sum(jnp.where(named, aligned, 0.0), axis=1, keepdims=True)
    inverse = jnp.sum(
        jnp.where((lane == 2 * top) | (lane == 2 * top + 1), meta, 0.0), axis=1, keepdims=True
    )
    r = lax.broadcasted_iota(jnp.int32, (rows, rows), 0)
    c = lax.broadcasted_iota(jnp.int32, (rows, rows), 1)
    shift = bits_of(block)
    before = jnp.where(((r >> shift) == (c >> shift)) & (c < r), 1.0, 0.0).astype(bf16)
    hits = jnp.broadcast_to(hit, (rows, LANES))
    slot = jnp.dot(before, hits.astype(bf16), preferred_element_type=f32)
    pos = lax.broadcasted_iota(jnp.int32, (rows, LANES), 0) >> shift
    sender = (relative_of(pos, order) ^ me).astype(f32)
    target = jnp.where(hits > 0.5, slot * senders + sender, -1.0)
    target_row = jnp.transpose(target)[:1, :]
    wanted = lax.broadcasted_iota(jnp.int32, (slots, rows), 0).astype(f32)
    select = jnp.where(wanted == target_row, 1.0, 0.0).astype(bf16)
    slot_gate = jnp.dot(
        select,
        jnp.broadcast_to(gate, (rows, LANES)).astype(bf16),
        preferred_element_type=f32,
    )[:, :1]

    for place in range(slabs):
        cols = slice(place * wide, (place + 1) * wide)
        both = []
        for kind in range(2):
            total = base_ref[kind, :, cols] + times_piece(
                x_ref, held_ref, window, copies, 2 * place + kind
            )
            if kind == 0:
                acc_ref[:, cols] = total
            both.append(total)
        gated = acc_ref[:, cols] * inverse
        act = (gated / (1.0 + jnp.exp(-gated)) * (both[1] * inverse)).astype(bf16)
        act_ref[:, cols] = jnp.dot(select, act, preferred_element_type=f32).astype(bf16)

    out_copies = []
    for j in range(tiles):
        cols = slice(j * tile, (j + 1) * tile)
        window.take()
        total = jnp.dot(act_ref[...], down_ref[:, cols], preferred_element_type=f32)
        out_ref[:, cols] = (total * slot_gate).astype(bf16)
        copy = pltpu.make_async_copy(out_ref.at[:, cols], out_hbm.at[:, cols], out_sems.at[j])
        copy.start()
        out_copies.append(copy)
    for copy in out_copies:
        copy.wait()


def in_vmem():
    return pl.BlockSpec(memory_space=pltpu.VMEM)


def in_any():
    return pl.BlockSpec(memory_space=pl.ANY)


def gate_up(a, b, gates, ups):
    half, columns = a[0].shape
    rows = 2 * half
    pieces = [w for pair in zip(gates, ups) for w in pair]
    wide = pieces[0].shape[2]
    hidden = wide * len(gates)
    return pl.pallas_call(
        functools.partial(gate_up_kernel, len(gates), rows // 4, columns),
        in_specs=[in_vmem()] * 4 + [in_any()] * len(pieces),
        out_specs=in_vmem(),
        out_shape=jax.ShapeDtypeStruct((2, rows, hidden), f32),
        scratch_shapes=[
            pltpu.VMEM((rows, 2 * columns), bf16),
            pltpu.VMEM((len(pieces), 2 * columns, wide), bf16),
            pltpu.SemaphoreType.DMA((len(pieces) + 1,)),
        ],
        compiler_params=pltpu.CompilerParams(vmem_limit_bytes=20 << 20),
        cost_estimate=pl.CostEstimate(
            flops=8 * rows * columns * hidden,
            bytes_accessed=8 * columns * hidden + 8 * rows * hidden,
            transcendentals=0,
        ),
        name="gate_up",
    )(*a, *b, *map(in_hbm, pieces))


def finish(place, a, b, base, gates, ups, downs, first_row, block, order, top, senders, capacity):
    half, columns = a[0].shape
    rows = 2 * half
    pieces = [w for pair in zip(gates, ups) for w in pair]
    wide = pieces[0].shape[2]
    hidden = wide * len(gates)
    width = downs[0].shape[2]
    tiles = width // column_tile(width, 1024)
    slots = senders * capacity
    return pl.pallas_call(
        functools.partial(
            finish_kernel, len(gates), rows // 4, columns, first_row, block, order, top, senders
        ),
        in_specs=[pl.BlockSpec(memory_space=pltpu.SMEM)]
        + [in_vmem()] * 5
        + [in_any()] * (len(pieces) + len(downs)),
        out_specs=in_any(),
        out_shape=jax.ShapeDtypeStruct((slots, width), bf16),
        scratch_shapes=[
            pltpu.VMEM((rows, 2 * columns), bf16),
            pltpu.VMEM((len(pieces), 2 * columns, wide), bf16),
            pltpu.VMEM((rows, hidden), f32),
            pltpu.VMEM((slots, hidden), bf16),
            pltpu.VMEM((hidden, width), bf16),
            pltpu.VMEM((slots, width), bf16),
            pltpu.SemaphoreType.DMA((len(pieces) + 1,)),
            pltpu.SemaphoreType.DMA((tiles, len(downs))),
            pltpu.SemaphoreType.DMA((tiles,)),
        ],
        compiler_params=pltpu.CompilerParams(vmem_limit_bytes=42 << 20),
        cost_estimate=pl.CostEstimate(
            flops=8 * rows * columns * hidden + 2 * slots * hidden * width,
            bytes_accessed=8 * columns * hidden + 2 * hidden * width + 2 * slots * width,
            transcendentals=rows * hidden,
        ),
        name="finish",
    )(place, *a, *b, base, *map(in_hbm, pieces + downs))


def add(a, b):
    return (a.astype(f32) + b.astype(f32)).astype(bf16)


def swap(value, bit, count):
    return lax.ppermute(value, "exp", [(i, i ^ (1 << bit)) for i in range(count)])


def shifted(value, count):
    return [value] + [
        lax.ppermute(value, "ctx", [(i, (i + k) % count) for i in range(count)])
        for k in range(1, count)
    ]


def tie(*values):
    return lax.optimization_barrier(values)


def first_swap(parts, count):
    _, send_a, _, send_b = parts
    return swap(send_a, 0, count), swap(send_b, 1, count)


def second_swap(parts, got, count):
    keep_a, _, keep_b, _ = parts
    got_a, got_b = got
    half = keep_a.shape[0] // 2
    next_a = add(keep_a[half:], got_a[half:])
    next_b = add(keep_b[half:], got_b[half:])
    got_a2, got_b2 = swap(next_a, 1, count), swap(next_b, 0, count)
    keep_a = add(keep_a[:half], got_a[:half])
    keep_b = add(keep_b[:half], got_b[:half])
    return keep_a, keep_b, got_a2, got_b2


def joined(terms):
    keep_a, keep_b, got_a, got_b = terms
    return (
        jnp.concatenate([keep_a, keep_b], axis=1),
        jnp.concatenate([got_a, got_b], axis=1),
    )


def halve(terms, bit, count):
    keep, got = terms
    half = keep.shape[0] // 2
    arrived = swap(add(keep[half:], got[half:]), bit, count)
    return add(keep[:half], got[:half]), arrived


def double(rows, bit, count):
    return jnp.concatenate([rows, swap(rows, bit, count)], axis=0)


def gather_half(rows, split, count):
    return double(rows[:, :split], 1, count), double(rows[:, split:], 0, count)


def gather_last(low, count):
    low_a, low_b = low
    return [low_a, swap(low_a, 0, count)], [low_b, swap(low_b, 1, count)]


def body(
    queries, latent, value_up, out_proj, residual, norm_gain, routes, gates, w_gate, w_up, w_down
):
    slabs = lax.axis_size("ctx")
    senders = lax.axis_size("exp")
    bits = bits_of(senders)
    block, width = residual.shape
    top = routes.shape[1]
    expert_count = senders * w_gate.shape[0]
    capacity = max(2, 3 * block * top // (2 * expert_count))
    orders = (list(range(bits)), [1, 0, *range(2, bits)])
    tiles = width // (2 * LANES)
    low = LANES * (tiles * first_share // 28)
    halves = (low, LANES * tiles - low)
    place = jnp.stack([lax.axis_index("ctx"), lax.axis_index("exp")]).astype(jnp.int32)

    keys = shifted(latent.T, slabs)
    arrived, gate_source, up_source = tie(keys[1:], w_gate, w_up)
    keys = [keys[0], *arrived]
    gate_others = shifted(gate_source, slabs)[1:]
    up_others = shifted(up_source, slabs)[1:]

    hva, hvb, *parts = attend_project(
        place, queries, keys, value_up, out_proj, halves[0], block, orders
    )
    more = project_more(hva, hvb, out_proj, 2 * halves[0], halves[1])
    gain = norm_gain.astype(f32)
    inner_bits = list(range(2, bits))

    def finished(terms, c):
        keep, got = terms
        cols = slice(2 * halves[0] * c, 2 * (halves[0] + halves[1] * c))
        rows = (residual[:, cols].astype(f32) + (keep.astype(f32) + got.astype(f32))).astype(bf16)
        wide = rows.astype(f32)
        return (
            rows,
            (wide * gain[None, cols]).astype(bf16),
            jnp.sum(wide * wide, axis=1, keepdims=True),
        )

    got = first_swap(parts, senders)
    got, more, gate_others = tie(got, more, gate_others)
    terms = second_swap(parts, got, senders)
    got = first_swap(more, senders)
    ahead, rest = joined(terms), inner_bits[:-1]
    for bit in rest:
        ahead = halve(ahead, bit, senders)
    got, _, up_others, down_source = tie(got, ahead, up_others, w_down)
    down_others = shifted(down_source, slabs)[1:]

    behind = second_swap(more, got, senders)
    ahead = halve(ahead, inner_bits[-1], senders)
    hidden_0, payload, squares_0 = finished(ahead, 0)
    behind = joined(behind)
    for bit in inner_bits[:-1]:
        behind = halve(behind, bit, senders)
    payload = double(payload, inner_bits[-1], senders)
    behind = halve(behind, inner_bits[-1], senders)
    for bit in inner_bits[-2::-1]:
        payload = double(payload, bit, senders)
    behind, down_others = tie(behind, down_others)
    hidden_1, rows, squares_1 = finished(behind, 1)
    inverse = lax.rsqrt((squares_0 + squares_1) / width + norm_epsilon)
    coarse = lax.reduce_precision(inverse, 8, 7)
    meta = jnp.concatenate(
        [
            routes.astype(bf16),
            gates.astype(bf16),
            coarse.astype(bf16),
            (inverse - coarse).astype(bf16),
            jnp.zeros((block, LANES - 2 * top - 2), bf16),
        ],
        axis=1,
    )
    rows = jnp.concatenate([rows, meta], axis=1)

    gate_parts = [w_gate, *gate_others]
    up_parts = [w_up, *up_others]
    down_parts = [w_down, *down_others]
    low = gather_half(payload, halves[0], senders)
    for bit in inner_bits[::-1]:
        rows = double(rows, bit, senders)
    a, b = gather_last(low, senders)
    low = gather_half(rows, halves[1], senders)
    a, b, low = tie(a, b, low)
    base = gate_up(a, b, gate_parts, up_parts)
    a, b = gather_last(low, senders)
    slots = finish(
        place, a, b, base, gate_parts, up_parts, down_parts, 2 * halves[0], block, orders[0], top, senders, capacity
    )
    expert_out = slots.reshape(capacity, senders, width).transpose(1, 0, 2)[None, None]
    return jnp.concatenate([hidden_0, hidden_1], axis=1), expert_out


def solution(mesh):
    placed = (
        P("ctx", "exp"),
        P("ctx", None),
        P("exp", None, None),
        P("exp", None),
        P(("ctx", "exp"), None),
        P(),
        P(("ctx", "exp"), None),
        P(("ctx", "exp"), None),
        P("exp", None, "ctx"),
        P("exp", None, "ctx"),
        P("exp", "ctx", None),
    )
    return jax.shard_map(
        body,
        mesh=mesh,
        in_specs=placed,
        out_specs=(P(("ctx", "exp"), None), P("ctx", "exp", None, None, None)),
        check_vma=False,
    )
```

```python
import functools
import math

import jax
import jax.numpy as jnp
from jax import lax
from jax.experimental import pallas as pl
from jax.experimental.pallas import tpu as pltpu
from jax.sharding import PartitionSpec as P

score_scale = 192.0 ** (-0.5)
norm_epsilon = 1e-06
masked_value = -1e30
LANES = 128
first_share = 16
f32 = jnp.float32
bf16 = jnp.bfloat16


def bits_of(count):
    return count.bit_length() - 1


def relative_of(pos, order):
    rel = jnp.zeros_like(pos)
    for i, bit in enumerate(order):
        rel = rel | (((pos >> (len(order) - 1 - i)) & 1) << bit)
    return rel


def order_matrix(rows, block, order, me):
    shift = bits_of(block)
    row = lax.broadcasted_iota(jnp.int32, (rows, rows), 0)
    col = lax.broadcasted_iota(jnp.int32, (rows, rows), 1)
    source = ((relative_of(row >> shift, order) ^ me) << shift) | (row & (block - 1))
    return jnp.where(col == source, 1.0, 0.0).astype(bf16)


def attend_kernel(
    slabs, block, orders, place_ref, q_ref, *refs
):
    keys = refs[:slabs]
    up_ref, wa_ref, wb_ref = refs[slabs : slabs + 3]
    hva_ref, hvb_ref, ka_ref, sa_ref, kb_ref, sb_ref = refs[slabs + 3 : slabs + 9]
    padded_ref, hv_ref = refs[slabs + 9 :]
    heads, latent_width, value_width = up_ref.shape
    qk, slab = keys[0].shape
    rows = q_ref.shape[0]
    span = slab * slabs

    @pl.when(pl.program_id(0) == 0)
    def _():
        here = place_ref[0]
        me = place_ref[1]
        offsets = sorted({(h * qk) % LANES for h in range(heads)})
        padded_ref[...] = jnp.zeros_like(padded_ref)
        for n, offset in enumerate(offsets):
            for k in range(slabs):
                padded_ref[n, offset : offset + qk, k * slab : (k + 1) * slab] = keys[k][...]
        col = lax.broadcasted_iota(jnp.int32, (rows, span), 1)
        key_pos = col
        for k in range(slabs):
            base = lax.rem(here - k + slabs, slabs) * slab
            key_pos = jnp.where(col >= k * slab, col - k * slab + base, key_pos)
        query_pos = lax.broadcasted_iota(jnp.int32, (rows, span), 0) + here * slab
        visible = (key_pos <= query_pos) & (key_pos > query_pos - span // 2)
        for h in range(heads):
            offset = (h * qk) % LANES
            start = h * qk - offset
            width = -(-(offset + qk) // LANES) * LANES
            n = offsets.index(offset)
            scores = (
                jnp.dot(
                    q_ref[:, start : start + width],
                    padded_ref[n, :width, :],
                    preferred_element_type=f32,
                )
                * score_scale
            )
            masked = jnp.where(visible, scores, masked_value)
            top = jnp.max(masked, axis=1, keepdims=True)
            weights = jnp.where(visible, jnp.exp(masked - top), 0.0)
            total = jnp.sum(weights, axis=1, keepdims=True)
            mixed = lax.dot_general(
                weights.astype(bf16),
                padded_ref[0, :latent_width, :],
                (((1,), (1,)), ((), ())),
                preferred_element_type=f32,
            )
            attended = (mixed / total).astype(bf16)
            hv_ref[:, h * value_width : (h + 1) * value_width] = jnp.dot(
                attended, up_ref[h], preferred_element_type=f32
            ).astype(bf16)
        hv = hv_ref[...]
        for out_ref, order in zip((hva_ref, hvb_ref), orders):
            out_ref[...] = jnp.dot(
                order_matrix(rows, block, order, me), hv, preferred_element_type=f32
            ).astype(bf16)

    project(hva_ref, wa_ref, ka_ref, sa_ref)
    project(hvb_ref, wb_ref, kb_ref, sb_ref)


def project(hv_ref, w_ref, keep_ref, send_ref):
    half = keep_ref.shape[0]
    out = jnp.dot(hv_ref[...], w_ref[...], preferred_element_type=f32).astype(bf16)
    keep_ref[...] = out[:half]
    send_ref[...] = out[half:]


def project_kernel(hva_ref, hvb_ref, wa_ref, wb_ref, ka_ref, sa_ref, kb_ref, sb_ref):
    project(hva_ref, wa_ref, ka_ref, sa_ref)
    project(hvb_ref, wb_ref, kb_ref, sb_ref)


def in_hbm(value):
    return pltpu.with_memory_space_constraint(value, pltpu.HBM)


def column_tile(columns, most):
    tiles = columns // LANES
    return LANES * max(t for t in range(1, tiles + 1) if tiles % t == 0 and t * LANES <= most)


def project_specs(rows, inner, first, half):
    tile = column_tile(math.gcd(first, half), 1024)
    steps = half // tile
    weights = [
        pl.BlockSpec((inner, tile), lambda i, at=at: (0, at + i))
        for at in (first // tile, first // tile + steps)
    ]
    outs = [pl.BlockSpec((rows // 2, tile), lambda i: (0, i))] * 4
    shapes = [jax.ShapeDtypeStruct((rows // 2, half), bf16)] * 4
    return steps, weights, outs, shapes


def whole(shape):
    return pl.BlockSpec(shape, lambda i: (0,) * len(shape))


def attend_project(place, queries, keys, value_up, out_proj, half, block, orders):
    rows, _ = queries.shape
    heads, _, value_width = value_up.shape
    qk, slab = keys[0].shape
    slabs = len(keys)
    span = slab * slabs
    inner = out_proj.shape[0]
    steps, weights, outs, shapes = project_specs(rows, inner, 0, half)
    offsets = {(h * qk) % LANES for h in range(heads)}
    deep = max(-(-(o + qk) // LANES) * LANES for o in offsets)
    flops = 2 * rows * (heads * span * 2 * qk + inner * 2 * half)
    return pl.pallas_call(
        functools.partial(attend_kernel, slabs, block, orders),
        grid=(steps,),
        in_specs=[
            pl.BlockSpec(memory_space=pltpu.SMEM),
            whole(queries.shape),
            *[whole(k.shape) for k in keys],
            whole(value_up.shape),
            *weights,
        ],
        out_specs=[whole((rows, inner))] * 2 + outs,
        out_shape=[jax.ShapeDtypeStruct((rows, inner), bf16)] * 2 + shapes,
        scratch_shapes=[
            pltpu.VMEM((len(offsets), deep, span), bf16),
            pltpu.VMEM((rows, inner), bf16),
        ],
        compiler_params=pltpu.CompilerParams(vmem_limit_bytes=24 << 20),
        cost_estimate=pl.CostEstimate(
            flops=flops,
            bytes_accessed=4 * (inner + rows) * half + queries.size * 2,
            transcendentals=rows * span * heads,
        ),
        name="attend_project",
    )(place, in_hbm(queries), in_hbm(keys[0]), *keys[1:], in_hbm(value_up), in_hbm(out_proj), in_hbm(out_proj))


def project_more(hva, hvb, out_proj, first, half):
    rows, inner = hva.shape
    steps, weights, outs, shapes = project_specs(rows, inner, first, half)
    return pl.pallas_call(
        project_kernel,
        grid=(steps,),
        in_specs=[whole(hva.shape), whole(hvb.shape), *weights],
        out_specs=outs,
        out_shape=shapes,
        compiler_params=pltpu.CompilerParams(vmem_limit_bytes=16 << 20),
        cost_estimate=pl.CostEstimate(
            flops=4 * rows * inner * half,
            bytes_accessed=4 * (inner + rows) * half,
            transcendentals=0,
        ),
        name="project_more",
    )(hva, hvb, in_hbm(out_proj), in_hbm(out_proj))


def place_rows(quarter_rows, columns, a_refs, b_refs, x_ref):
    a_low, a_high = a_refs
    b_low, b_high = b_refs
    q = quarter_rows
    for ref, source, count, target, first in (
        (a_low, 0, 2 * q, 0, 0),
        (a_high, 0, 2 * q, 2 * q, 0),
        (b_low, 0, q, 0, columns),
        (b_low, q, q, 2 * q, columns),
        (b_high, 0, q, q, columns),
        (b_high, q, q, 3 * q, columns),
    ):
        x_ref[target : target + count, first : first + columns] = ref[
            source : source + count, :columns
        ]


def weight_copies(pieces, held_ref, sems, first_row):
    deep = held_ref.shape[1]
    copies = []
    for p, w_ref in enumerate(pieces):
        cuts = (0, deep // 2, deep) if p == 0 else (0, deep)
        for n, (low, high) in enumerate(zip(cuts, cuts[1:])):
            copy = pltpu.make_async_copy(
                w_ref.at[0, first_row + low : first_row + high, :],
                held_ref.at[p, low:high, :],
                sems.at[p + (n if p == 0 else 1)],
            )
            copies.append((p, low, high, [copy]))
    return copies


class Window:
    def __init__(self, groups, ahead):
        self.groups, self.ahead, self.used = groups, ahead, 0
        for group in groups[:ahead]:
            self.start(group)

    def start(self, group):
        for copy in group:
            copy.start()

    def take(self):
        for copy in self.groups[self.used]:
            copy.wait()
        if self.used + self.ahead < len(self.groups):
            self.start(self.groups[self.used + self.ahead])
        self.used += 1


def times_piece(x_ref, held_ref, window, copies, piece):
    total = None
    for p, low, high, _ in copies:
        if p == piece:
            window.take()
            term = jnp.dot(x_ref[:, low:high], held_ref[p, low:high, :], preferred_element_type=f32)
            total = term if total is None else total + term
    return total


def gate_up_kernel(slabs, quarter_rows, columns, *refs):
    a_refs, b_refs = refs[:2], refs[2:4]
    pieces = refs[4 : 4 + 2 * slabs]
    acc_ref, x_ref, held_ref, sems = refs[4 + 2 * slabs :]
    copies = weight_copies(pieces, held_ref, sems, 0)
    window = Window([c[3] for c in copies], 3)
    place_rows(quarter_rows, columns, a_refs, b_refs, x_ref)
    wide = held_ref.shape[2]
    for p in range(len(pieces)):
        place, kind = divmod(p, 2)
        acc_ref[kind, :, place * wide : (place + 1) * wide] = times_piece(
            x_ref, held_ref, window, copies, p
        )


def finish_kernel(slabs, quarter_rows, columns, first_row, block, order, top, senders, place_ref, *refs):
    a_refs, b_refs = refs[:2], refs[2:4]
    base_ref = refs[4]
    pieces = refs[5 : 5 + 2 * slabs]
    downs = refs[5 + 2 * slabs : 5 + 3 * slabs]
    (out_hbm, x_ref, held_ref, acc_ref, act_ref, down_ref, out_ref, sems, down_sems, out_sems) = refs[
        5 + 3 * slabs :
    ]
    rows = 4 * quarter_rows
    q = quarter_rows
    slots, width = out_ref.shape
    part = downs[0].shape[1]
    wide = held_ref.shape[2]
    tiles = down_sems.shape[0]
    tile = width // tiles
    copies = weight_copies(pieces, held_ref, sems, first_row)
    down_copies = [
        [
            pltpu.make_async_copy(
                w_ref.at[0, :, j * tile : (j + 1) * tile],
                down_ref.at[p * part : (p + 1) * part, j * tile : (j + 1) * tile],
                down_sems.at[j, p],
            )
            for p, w_ref in enumerate(downs)
        ]
        for j in range(tiles)
    ]
    window = Window([c[3] for c in copies] + down_copies, 3)
    place_rows(quarter_rows, columns, a_refs, b_refs, x_ref)

    me = place_ref[1]
    b_low, b_high = b_refs
    meta = jnp.concatenate(
        [b_low[:q, columns:], b_high[:q, columns:], b_low[q:, columns:], b_high[q:, columns:]],
        axis=0,
    ).astype(f32)
    lane = lax.broadcasted_iota(jnp.int32, (rows, LANES), 1)
    named = (lane < top) & (meta == me.astype(f32))
    hit = jnp.max(jnp.where(named, 1.0, 0.0), axis=1, keepdims=True)
    aligned = pltpu.roll(meta, LANES - top, 1)
    gate = jnp.sum(jnp.where(named, aligned, 0.0), axis=1, keepdims=True)
    inverse = jnp.sum(
        jnp.where((lane == 2 * top) | (lane == 2 * top + 1), meta, 0.0), axis=1, keepdims=True
    )
    r = lax.broadcasted_iota(jnp.int32, (rows, rows), 0)
    c = lax.broadcasted_iota(jnp.int32, (rows, rows), 1)
    shift = bits_of(block)
    before = jnp.where(((r >> shift) == (c >> shift)) & (c < r), 1.0, 0.0).astype(bf16)
    hits = jnp.broadcast_to(hit, (rows, LANES))
    slot = jnp.dot(before, hits.astype(bf16), preferred_element_type=f32)
    pos = lax.broadcasted_iota(jnp.int32, (rows, LANES), 0) >> shift
    sender = (relative_of(pos, order) ^ me).astype(f32)
    target = jnp.where(hits > 0.5, slot * senders + sender, -1.0)
    target_row = jnp.transpose(target)[:1, :]
    wanted = lax.broadcasted_iota(jnp.int32, (slots, rows), 0).astype(f32)
    select = jnp.where(wanted == target_row, 1.0, 0.0).astype(bf16)
    slot_gate = jnp.dot(
        select,
        jnp.broadcast_to(gate, (rows, LANES)).astype(bf16),
        preferred_element_type=f32,
    )[:, :1]

    for place in range(slabs):
        cols = slice(place * wide, (place + 1) * wide)
        both = []
        for kind in range(2):
            total = base_ref[kind, :, cols] + times_piece(
                x_ref, held_ref, window, copies, 2 * place + kind
            )
            if kind == 0:
                acc_ref[:, cols] = total
            both.append(total)
        gated = acc_ref[:, cols] * inverse
        act = (gated / (1.0 + jnp.exp(-gated)) * (both[1] * inverse)).astype(bf16)
        act_ref[:, cols] = jnp.dot(select, act, preferred_element_type=f32).astype(bf16)

    out_copies = []
    for j in range(tiles):
        cols = slice(j * tile, (j + 1) * tile)
        window.take()
        total = jnp.dot(act_ref[...], down_ref[:, cols], preferred_element_type=f32)
        out_ref[:, cols] = (total * slot_gate).astype(bf16)
        copy = pltpu.make_async_copy(out_ref.at[:, cols], out_hbm.at[:, cols], out_sems.at[j])
        copy.start()
        out_copies.append(copy)
    for copy in out_copies:
        copy.wait()


def in_vmem():
    return pl.BlockSpec(memory_space=pltpu.VMEM)


def in_any():
    return pl.BlockSpec(memory_space=pl.ANY)


def gate_up(a, b, gates, ups):
    half, columns = a[0].shape
    rows = 2 * half
    pieces = [w for pair in zip(gates, ups) for w in pair]
    wide = pieces[0].shape[2]
    hidden = wide * len(gates)
    return pl.pallas_call(
        functools.partial(gate_up_kernel, len(gates), rows // 4, columns),
        in_specs=[in_vmem()] * 4 + [in_any()] * len(pieces),
        out_specs=in_vmem(),
        out_shape=jax.ShapeDtypeStruct((2, rows, hidden), f32),
        scratch_shapes=[
            pltpu.VMEM((rows, 2 * columns), bf16),
            pltpu.VMEM((len(pieces), 2 * columns, wide), bf16),
            pltpu.SemaphoreType.DMA((len(pieces) + 1,)),
        ],
        compiler_params=pltpu.CompilerParams(vmem_limit_bytes=24 << 20),
        cost_estimate=pl.CostEstimate(
            flops=8 * rows * columns * hidden,
            bytes_accessed=8 * columns * hidden + 8 * rows * hidden,
            transcendentals=0,
        ),
        name="gate_up",
    )(*a, *b, *map(in_hbm, pieces))


def finish(place, a, b, base, gates, ups, downs, first_row, block, order, top, senders, capacity):
    half, columns = a[0].shape
    rows = 2 * half
    pieces = [w for pair in zip(gates, ups) for w in pair]
    wide = pieces[0].shape[2]
    hidden = wide * len(gates)
    width = downs[0].shape[2]
    tiles = width // column_tile(width, 1024)
    slots = senders * capacity
    return pl.pallas_call(
        functools.partial(
            finish_kernel, len(gates), rows // 4, columns, first_row, block, order, top, senders
        ),
        in_specs=[pl.BlockSpec(memory_space=pltpu.SMEM)]
        + [in_vmem()] * 5
        + [in_any()] * (len(pieces) + len(downs)),
        out_specs=in_any(),
        out_shape=jax.ShapeDtypeStruct((slots, width), bf16),
        scratch_shapes=[
            pltpu.VMEM((rows, 2 * columns), bf16),
            pltpu.VMEM((len(pieces), 2 * columns, wide), bf16),
            pltpu.VMEM((rows, hidden), f32),
            pltpu.VMEM((slots, hidden), bf16),
            pltpu.VMEM((hidden, width), bf16),
            pltpu.VMEM((slots, width), bf16),
            pltpu.SemaphoreType.DMA((len(pieces) + 1,)),
            pltpu.SemaphoreType.DMA((tiles, len(downs))),
            pltpu.SemaphoreType.DMA((tiles,)),
        ],
        compiler_params=pltpu.CompilerParams(vmem_limit_bytes=42 << 20),
        cost_estimate=pl.CostEstimate(
            flops=8 * rows * columns * hidden + 2 * slots * hidden * width,
            bytes_accessed=8 * columns * hidden + 2 * hidden * width + 2 * slots * width,
            transcendentals=rows * hidden,
        ),
        name="finish",
    )(place, *a, *b, base, *map(in_hbm, pieces + downs))


def add(a, b):
    return (a.astype(f32) + b.astype(f32)).astype(bf16)


def swap(value, bit, count):
    return lax.ppermute(value, "exp", [(i, i ^ (1 << bit)) for i in range(count)])


def shifted(value, count):
    return [value] + [
        lax.ppermute(value, "ctx", [(i, (i + k) % count) for i in range(count)])
        for k in range(1, count)
    ]


def tie(*values):
    return lax.optimization_barrier(values)


def first_swap(parts, count):
    _, send_a, _, send_b = parts
    return swap(send_a, 0, count), swap(send_b, 1, count)


def second_swap(parts, got, count):
    keep_a, _, keep_b, _ = parts
    got_a, got_b = got
    half = keep_a.shape[0] // 2
    next_a = add(keep_a[half:], got_a[half:])
    next_b = add(keep_b[half:], got_b[half:])
    got_a2, got_b2 = swap(next_a, 1, count), swap(next_b, 0, count)
    keep_a = add(keep_a[:half], got_a[:half])
    keep_b = add(keep_b[:half], got_b[:half])
    return keep_a, keep_b, got_a2, got_b2


def joined(terms):
    keep_a, keep_b, got_a, got_b = terms
    return (
        jnp.concatenate([keep_a, keep_b], axis=1),
        jnp.concatenate([got_a, got_b], axis=1),
    )


def halve(terms, bit, count):
    keep, got = terms
    half = keep.shape[0] // 2
    arrived = swap(add(keep[half:], got[half:]), bit, count)
    return add(keep[:half], got[:half]), arrived


def double(rows, bit, count):
    return jnp.concatenate([rows, swap(rows, bit, count)], axis=0)


def gather_half(rows, split, count):
    return double(rows[:, :split], 1, count), double(rows[:, split:], 0, count)


def gather_last(low, count):
    low_a, low_b = low
    return [low_a, swap(low_a, 0, count)], [low_b, swap(low_b, 1, count)]


def body(
    queries, latent, value_up, out_proj, residual, norm_gain, routes, gates, w_gate, w_up, w_down
):
    slabs = lax.axis_size("ctx")
    senders = lax.axis_size("exp")
    bits = bits_of(senders)
    block, width = residual.shape
    top = routes.shape[1]
    expert_count = senders * w_gate.shape[0]
    capacity = max(2, 3 * block * top // (2 * expert_count))
    orders = (list(range(bits)), [1, 0, *range(2, bits)])
    tiles = width // (2 * LANES)
    low = LANES * (tiles * first_share // 28)
    halves = (low, LANES * tiles - low)
    place = jnp.stack([lax.axis_index("ctx"), lax.axis_index("exp")]).astype(jnp.int32)

    keys = shifted(latent.T, slabs)
    arrived, gate_source, up_source = tie(keys[1:], w_gate, w_up)
    keys = [keys[0], *arrived]
    gate_others = shifted(gate_source, slabs)[1:]
    up_others = shifted(up_source, slabs)[1:]

    hva, hvb, *parts = attend_project(
        place, queries, keys, value_up, out_proj, halves[0], block, orders
    )
    more = project_more(hva, hvb, out_proj, 2 * halves[0], halves[1])
    gain = norm_gain.astype(f32)
    inner_bits = list(range(2, bits))

    def finished(terms, c):
        keep, got = terms
        cols = slice(2 * halves[0] * c, 2 * (halves[0] + halves[1] * c))
        rows = (residual[:, cols].astype(f32) + (keep.astype(f32) + got.astype(f32))).astype(bf16)
        wide = rows.astype(f32)
        return (
            rows,
            (wide * gain[None, cols]).astype(bf16),
            jnp.sum(wide * wide, axis=1, keepdims=True),
        )

    got = first_swap(parts, senders)
    got, more, gate_others, up_others, down_source = tie(got, more, gate_others, up_others, w_down)
    terms = second_swap(parts, got, senders)
    got = first_swap(more, senders)
    ahead, rest = joined(terms), inner_bits[:-1]
    for bit in rest:
        ahead = halve(ahead, bit, senders)
    got, _ = tie(got, ahead)
    down_others = shifted(down_source, slabs)[1:]

    behind = second_swap(more, got, senders)
    ahead = halve(ahead, inner_bits[-1], senders)
    hidden_0, payload, squares_0 = finished(ahead, 0)
    behind = joined(behind)
    for bit in inner_bits[:-1]:
        behind = halve(behind, bit, senders)
    payload = double(payload, inner_bits[-1], senders)
    behind = halve(behind, inner_bits[-1], senders)
    for bit in inner_bits[-2::-1]:
        payload = double(payload, bit, senders)
    behind, down_others = tie(behind, down_others)
    hidden_1, rows, squares_1 = finished(behind, 1)
    inverse = lax.rsqrt((squares_0 + squares_1) / width + norm_epsilon)
    coarse = lax.reduce_precision(inverse, 8, 7)
    meta = jnp.concatenate(
        [
            routes.astype(bf16),
            gates.astype(bf16),
            coarse.astype(bf16),
            (inverse - coarse).astype(bf16),
            jnp.zeros((block, LANES - 2 * top - 2), bf16),
        ],
        axis=1,
    )
    rows = jnp.concatenate([rows, meta], axis=1)

    gate_parts = [w_gate, *gate_others]
    up_parts = [w_up, *up_others]
    down_parts = [w_down, *down_others]
    low = gather_half(payload, halves[0], senders)
    for bit in inner_bits[::-1]:
        rows = double(rows, bit, senders)
    a, b = gather_last(low, senders)
    low = gather_half(rows, halves[1], senders)
    a, b, low = tie(a, b, low)
    base = gate_up(a, b, gate_parts, up_parts)
    a, b = gather_last(low, senders)
    slots = finish(
        place, a, b, base, gate_parts, up_parts, down_parts, 2 * halves[0], block, orders[0], top, senders, capacity
    )
    expert_out = slots.reshape(capacity, senders, width).transpose(1, 0, 2)[None, None]
    return jnp.concatenate([hidden_0, hidden_1], axis=1), expert_out


def solution(mesh):
    placed = (
        P("ctx", "exp"),
        P("ctx", None),
        P("exp", None, None),
        P("exp", None),
        P(("ctx", "exp"), None),
        P(),
        P(("ctx", "exp"), None),
        P(("ctx", "exp"), None),
        P("exp", None, "ctx"),
        P("exp", None, "ctx"),
        P("exp", "ctx", None),
    )
    return jax.shard_map(
        body,
        mesh=mesh,
        in_specs=placed,
        out_specs=(P(("ctx", "exp"), None), P("ctx", "exp", None, None, None)),
        check_vma=False,
    )
```

```python
import functools
import math

import jax
import jax.numpy as jnp
from jax import lax
from jax.experimental import pallas as pl
from jax.experimental.pallas import tpu as pltpu
from jax.sharding import PartitionSpec as P

score_scale = 192.0 ** (-0.5)
norm_epsilon = 1e-06
masked_value = -1e30
LANES = 128
first_share = 16
f32 = jnp.float32
bf16 = jnp.bfloat16


def bits_of(count):
    return count.bit_length() - 1


def relative_of(pos, order):
    rel = jnp.zeros_like(pos)
    for i, bit in enumerate(order):
        rel = rel | (((pos >> (len(order) - 1 - i)) & 1) << bit)
    return rel


def order_matrix(rows, block, order, me):
    shift = bits_of(block)
    row = lax.broadcasted_iota(jnp.int32, (rows, rows), 0)
    col = lax.broadcasted_iota(jnp.int32, (rows, rows), 1)
    source = ((relative_of(row >> shift, order) ^ me) << shift) | (row & (block - 1))
    return jnp.where(col == source, 1.0, 0.0).astype(bf16)


def attend_kernel(
    slabs, block, orders, place_ref, q_ref, *refs
):
    keys = refs[:slabs]
    up_ref, wa_ref, wb_ref = refs[slabs : slabs + 3]
    hva_ref, hvb_ref, ka_ref, sa_ref, kb_ref, sb_ref = refs[slabs + 3 : slabs + 9]
    padded_ref, hv_ref = refs[slabs + 9 :]
    heads, latent_width, value_width = up_ref.shape
    qk, slab = keys[0].shape
    rows = q_ref.shape[0]
    span = slab * slabs

    @pl.when(pl.program_id(0) == 0)
    def _():
        here = place_ref[0]
        me = place_ref[1]
        offsets = sorted({(h * qk) % LANES for h in range(heads)})
        padded_ref[...] = jnp.zeros_like(padded_ref)
        for n, offset in enumerate(offsets):
            for k in range(slabs):
                padded_ref[n, offset : offset + qk, k * slab : (k + 1) * slab] = keys[k][...]
        col = lax.broadcasted_iota(jnp.int32, (rows, span), 1)
        key_pos = col
        for k in range(slabs):
            base = lax.rem(here - k + slabs, slabs) * slab
            key_pos = jnp.where(col >= k * slab, col - k * slab + base, key_pos)
        query_pos = lax.broadcasted_iota(jnp.int32, (rows, span), 0) + here * slab
        visible = (key_pos <= query_pos) & (key_pos > query_pos - span // 2)
        for h in range(heads):
            offset = (h * qk) % LANES
            start = h * qk - offset
            width = -(-(offset + qk) // LANES) * LANES
            n = offsets.index(offset)
            scores = (
                jnp.dot(
                    q_ref[:, start : start + width],
                    padded_ref[n, :width, :],
                    preferred_element_type=f32,
                )
                * score_scale
            )
            masked = jnp.where(visible, scores, masked_value)
            top = jnp.max(masked, axis=1, keepdims=True)
            weights = jnp.where(visible, jnp.exp(masked - top), 0.0)
            total = jnp.sum(weights, axis=1, keepdims=True)
            mixed = lax.dot_general(
                weights.astype(bf16),
                padded_ref[0, :latent_width, :],
                (((1,), (1,)), ((), ())),
                preferred_element_type=f32,
            )
            attended = (mixed / total).astype(bf16)
            hv_ref[:, h * value_width : (h + 1) * value_width] = jnp.dot(
                attended, up_ref[h], preferred_element_type=f32
            ).astype(bf16)
        hv = hv_ref[...]
        for out_ref, order in zip((hva_ref, hvb_ref), orders):
            out_ref[...] = jnp.dot(
                order_matrix(rows, block, order, me), hv, preferred_element_type=f32
            ).astype(bf16)

    project(hva_ref, wa_ref, ka_ref, sa_ref)
    project(hvb_ref, wb_ref, kb_ref, sb_ref)


def project(hv_ref, w_ref, keep_ref, send_ref):
    half = keep_ref.shape[0]
    out = jnp.dot(hv_ref[...], w_ref[...], preferred_element_type=f32).astype(bf16)
    keep_ref[...] = out[:half]
    send_ref[...] = out[half:]


def project_kernel(hva_ref, hvb_ref, wa_ref, wb_ref, ka_ref, sa_ref, kb_ref, sb_ref):
    project(hva_ref, wa_ref, ka_ref, sa_ref)
    project(hvb_ref, wb_ref, kb_ref, sb_ref)


def in_hbm(value):
    return pltpu.with_memory_space_constraint(value, pltpu.HBM)


def column_tile(columns, most):
    tiles = columns // LANES
    return LANES * max(t for t in range(1, tiles + 1) if tiles % t == 0 and t * LANES <= most)


def project_specs(rows, inner, first, half):
    tile = column_tile(math.gcd(first, half), 1024)
    steps = half // tile
    weights = [
        pl.BlockSpec((inner, tile), lambda i, at=at: (0, at + i))
        for at in (first // tile, first // tile + steps)
    ]
    outs = [pl.BlockSpec((rows // 2, tile), lambda i: (0, i))] * 4
    shapes = [jax.ShapeDtypeStruct((rows // 2, half), bf16)] * 4
    return steps, weights, outs, shapes


def whole(shape):
    return pl.BlockSpec(shape, lambda i: (0,) * len(shape))


def attend_project(place, queries, keys, value_up, out_proj, half, block, orders):
    rows, _ = queries.shape
    heads, _, value_width = value_up.shape
    qk, slab = keys[0].shape
    slabs = len(keys)
    span = slab * slabs
    inner = out_proj.shape[0]
    steps, weights, outs, shapes = project_specs(rows, inner, 0, half)
    offsets = {(h * qk) % LANES for h in range(heads)}
    deep = max(-(-(o + qk) // LANES) * LANES for o in offsets)
    flops = 2 * rows * (heads * span * 2 * qk + inner * 2 * half)
    return pl.pallas_call(
        functools.partial(attend_kernel, slabs, block, orders),
        grid=(steps,),
        in_specs=[
            pl.BlockSpec(memory_space=pltpu.SMEM),
            whole(queries.shape),
            *[whole(k.shape) for k in keys],
            whole(value_up.shape),
            *weights,
        ],
        out_specs=[whole((rows, inner))] * 2 + outs,
        out_shape=[jax.ShapeDtypeStruct((rows, inner), bf16)] * 2 + shapes,
        scratch_shapes=[
            pltpu.VMEM((len(offsets), deep, span), bf16),
            pltpu.VMEM((rows, inner), bf16),
        ],
        compiler_params=pltpu.CompilerParams(vmem_limit_bytes=24 << 20),
        cost_estimate=pl.CostEstimate(
            flops=flops,
            bytes_accessed=4 * (inner + rows) * half + queries.size * 2,
            transcendentals=rows * span * heads,
        ),
        name="attend_project",
    )(place, in_hbm(queries), in_hbm(keys[0]), *keys[1:], in_hbm(value_up), in_hbm(out_proj), in_hbm(out_proj))


def project_more(hva, hvb, out_proj, first, half):
    rows, inner = hva.shape
    steps, weights, outs, shapes = project_specs(rows, inner, first, half)
    return pl.pallas_call(
        project_kernel,
        grid=(steps,),
        in_specs=[whole(hva.shape), whole(hvb.shape), *weights],
        out_specs=outs,
        out_shape=shapes,
        compiler_params=pltpu.CompilerParams(vmem_limit_bytes=16 << 20),
        cost_estimate=pl.CostEstimate(
            flops=4 * rows * inner * half,
            bytes_accessed=4 * (inner + rows) * half,
            transcendentals=0,
        ),
        name="project_more",
    )(hva, hvb, in_hbm(out_proj), in_hbm(out_proj))


def place_rows(quarter_rows, columns, a_refs, b_refs, x_ref):
    a_low, a_high = a_refs
    b_low, b_high = b_refs
    q = quarter_rows
    for ref, source, count, target, first in (
        (a_low, 0, 2 * q, 0, 0),
        (a_high, 0, 2 * q, 2 * q, 0),
        (b_low, 0, q, 0, columns),
        (b_low, q, q, 2 * q, columns),
        (b_high, 0, q, q, columns),
        (b_high, q, q, 3 * q, columns),
    ):
        x_ref[target : target + count, first : first + columns] = ref[
            source : source + count, :columns
        ]


def weight_copies(pieces, held_ref, sems, first_row):
    deep = held_ref.shape[1]
    copies = []
    for p, w_ref in enumerate(pieces):
        cuts = (0, deep // 2, deep) if p == 0 else (0, deep)
        for n, (low, high) in enumerate(zip(cuts, cuts[1:])):
            copy = pltpu.make_async_copy(
                w_ref.at[0, first_row + low : first_row + high, :],
                held_ref.at[p, low:high, :],
                sems.at[p + (n if p == 0 else 1)],
            )
            copies.append((p, low, high, [copy]))
    return copies


class Window:
    def __init__(self, groups, ahead):
        self.groups, self.ahead, self.used = groups, ahead, 0
        for group in groups[:ahead]:
            self.start(group)

    def start(self, group):
        for copy in group:
            copy.start()

    def take(self):
        for copy in self.groups[self.used]:
            copy.wait()
        if self.used + self.ahead < len(self.groups):
            self.start(self.groups[self.used + self.ahead])
        self.used += 1


def times_piece(x_ref, held_ref, window, copies, piece):
    total = None
    for p, low, high, _ in copies:
        if p == piece:
            window.take()
            term = jnp.dot(x_ref[:, low:high], held_ref[p, low:high, :], preferred_element_type=f32)
            total = term if total is None else total + term
    return total


def gate_up_kernel(slabs, quarter_rows, columns, *refs):
    a_refs, b_refs = refs[:2], refs[2:4]
    pieces = refs[4 : 4 + 2 * slabs]
    acc_ref, x_ref, held_ref, sems = refs[4 + 2 * slabs :]
    copies = weight_copies(pieces, held_ref, sems, 0)
    window = Window([c[3] for c in copies], 4)
    place_rows(quarter_rows, columns, a_refs, b_refs, x_ref)
    wide = held_ref.shape[2]
    for p in range(len(pieces)):
        place, kind = divmod(p, 2)
        acc_ref[kind, :, place * wide : (place + 1) * wide] = times_piece(
            x_ref, held_ref, window, copies, p
        )


def finish_kernel(slabs, quarter_rows, columns, first_row, block, order, top, senders, place_ref, *refs):
    a_refs, b_refs = refs[:2], refs[2:4]
    base_ref = refs[4]
    pieces = refs[5 : 5 + 2 * slabs]
    downs = refs[5 + 2 * slabs : 5 + 3 * slabs]
    (out_hbm, x_ref, held_ref, acc_ref, act_ref, down_ref, out_ref, sems, down_sems, out_sems) = refs[
        5 + 3 * slabs :
    ]
    rows = 4 * quarter_rows
    q = quarter_rows
    slots, width = out_ref.shape
    part = downs[0].shape[1]
    wide = held_ref.shape[2]
    tiles = down_sems.shape[0]
    tile = width // tiles
    copies = weight_copies(pieces, held_ref, sems, first_row)
    down_copies = [
        [
            pltpu.make_async_copy(
                w_ref.at[0, :, j * tile : (j + 1) * tile],
                down_ref.at[p * part : (p + 1) * part, j * tile : (j + 1) * tile],
                down_sems.at[j, p],
            )
            for p, w_ref in enumerate(downs)
        ]
        for j in range(tiles)
    ]
    window = Window([c[3] for c in copies] + down_copies, 4)
    place_rows(quarter_rows, columns, a_refs, b_refs, x_ref)

    me = place_ref[1]
    b_low, b_high = b_refs
    meta = jnp.concatenate(
        [b_low[:q, columns:], b_high[:q, columns:], b_low[q:, columns:], b_high[q:, columns:]],
        axis=0,
    ).astype(f32)
    lane = lax.broadcasted_iota(jnp.int32, (rows, LANES), 1)
    named = (lane < top) & (meta == me.astype(f32))
    hit = jnp.max(jnp.where(named, 1.0, 0.0), axis=1, keepdims=True)
    aligned = pltpu.roll(meta, LANES - top, 1)
    gate = jnp.sum(jnp.where(named, aligned, 0.0), axis=1, keepdims=True)
    inverse = jnp.sum(
        jnp.where((lane == 2 * top) | (lane == 2 * top + 1), meta, 0.0), axis=1, keepdims=True
    )
    r = lax.broadcasted_iota(jnp.int32, (rows, rows), 0)
    c = lax.broadcasted_iota(jnp.int32, (rows, rows), 1)
    shift = bits_of(block)
    before = jnp.where(((r >> shift) == (c >> shift)) & (c < r), 1.0, 0.0).astype(bf16)
    hits = jnp.broadcast_to(hit, (rows, LANES))
    slot = jnp.dot(before, hits.astype(bf16), preferred_element_type=f32)
    pos = lax.broadcasted_iota(jnp.int32, (rows, LANES), 0) >> shift
    sender = (relative_of(pos, order) ^ me).astype(f32)
    target = jnp.where(hits > 0.5, slot * senders + sender, -1.0)
    target_row = jnp.transpose(target)[:1, :]
    wanted = lax.broadcasted_iota(jnp.int32, (slots, rows), 0).astype(f32)
    select = jnp.where(wanted == target_row, 1.0, 0.0).astype(bf16)
    slot_gate = jnp.dot(
        select,
        jnp.broadcast_to(gate, (rows, LANES)).astype(bf16),
        preferred_element_type=f32,
    )[:, :1]

    for place in range(slabs):
        cols = slice(place * wide, (place + 1) * wide)
        both = []
        for kind in range(2):
            total = base_ref[kind, :, cols] + times_piece(
                x_ref, held_ref, window, copies, 2 * place + kind
            )
            if kind == 0:
                acc_ref[:, cols] = total
            both.append(total)
        gated = acc_ref[:, cols] * inverse
        act = (gated / (1.0 + jnp.exp(-gated)) * (both[1] * inverse)).astype(bf16)
        act_ref[:, cols] = jnp.dot(select, act, preferred_element_type=f32).astype(bf16)

    out_copies = []
    for j in range(tiles):
        cols = slice(j * tile, (j + 1) * tile)
        window.take()
        total = jnp.dot(act_ref[...], down_ref[:, cols], preferred_element_type=f32)
        out_ref[:, cols] = (total * slot_gate).astype(bf16)
        copy = pltpu.make_async_copy(out_ref.at[:, cols], out_hbm.at[:, cols], out_sems.at[j])
        copy.start()
        out_copies.append(copy)
    for copy in out_copies:
        copy.wait()


def in_vmem():
    return pl.BlockSpec(memory_space=pltpu.VMEM)


def in_any():
    return pl.BlockSpec(memory_space=pl.ANY)


def gate_up(a, b, gates, ups):
    half, columns = a[0].shape
    rows = 2 * half
    pieces = [w for pair in zip(gates, ups) for w in pair]
    wide = pieces[0].shape[2]
    hidden = wide * len(gates)
    return pl.pallas_call(
        functools.partial(gate_up_kernel, len(gates), rows // 4, columns),
        in_specs=[in_vmem()] * 4 + [in_any()] * len(pieces),
        out_specs=in_vmem(),
        out_shape=jax.ShapeDtypeStruct((2, rows, hidden), f32),
        scratch_shapes=[
            pltpu.VMEM((rows, 2 * columns), bf16),
            pltpu.VMEM((len(pieces), 2 * columns, wide), bf16),
            pltpu.SemaphoreType.DMA((len(pieces) + 1,)),
        ],
        compiler_params=pltpu.CompilerParams(vmem_limit_bytes=24 << 20),
        cost_estimate=pl.CostEstimate(
            flops=8 * rows * columns * hidden,
            bytes_accessed=8 * columns * hidden + 8 * rows * hidden,
            transcendentals=0,
        ),
        name="gate_up",
    )(*a, *b, *map(in_hbm, pieces))


def finish(place, a, b, base, gates, ups, downs, first_row, block, order, top, senders, capacity):
    half, columns = a[0].shape
    rows = 2 * half
    pieces = [w for pair in zip(gates, ups) for w in pair]
    wide = pieces[0].shape[2]
    hidden = wide * len(gates)
    width = downs[0].shape[2]
    tiles = width // column_tile(width, 1024)
    slots = senders * capacity
    return pl.pallas_call(
        functools.partial(
            finish_kernel, len(gates), rows // 4, columns, first_row, block, order, top, senders
        ),
        in_specs=[pl.BlockSpec(memory_space=pltpu.SMEM)]
        + [in_vmem()] * 5
        + [in_any()] * (len(pieces) + len(downs)),
        out_specs=in_any(),
        out_shape=jax.ShapeDtypeStruct((slots, width), bf16),
        scratch_shapes=[
            pltpu.VMEM((rows, 2 * columns), bf16),
            pltpu.VMEM((len(pieces), 2 * columns, wide), bf16),
            pltpu.VMEM((rows, hidden), f32),
            pltpu.VMEM((slots, hidden), bf16),
            pltpu.VMEM((hidden, width), bf16),
            pltpu.VMEM((slots, width), bf16),
            pltpu.SemaphoreType.DMA((len(pieces) + 1,)),
            pltpu.SemaphoreType.DMA((tiles, len(downs))),
            pltpu.SemaphoreType.DMA((tiles,)),
        ],
        compiler_params=pltpu.CompilerParams(vmem_limit_bytes=42 << 20),
        cost_estimate=pl.CostEstimate(
            flops=8 * rows * columns * hidden + 2 * slots * hidden * width,
            bytes_accessed=8 * columns * hidden + 2 * hidden * width + 2 * slots * width,
            transcendentals=rows * hidden,
        ),
        name="finish",
    )(place, *a, *b, base, *map(in_hbm, pieces + downs))


def add(a, b):
    return (a.astype(f32) + b.astype(f32)).astype(bf16)


def swap(value, bit, count):
    return lax.ppermute(value, "exp", [(i, i ^ (1 << bit)) for i in range(count)])


def shifted(value, count):
    return [value] + [
        lax.ppermute(value, "ctx", [(i, (i + k) % count) for i in range(count)])
        for k in range(1, count)
    ]


def tie(*values):
    return lax.optimization_barrier(values)


def first_swap(parts, count):
    _, send_a, _, send_b = parts
    return swap(send_a, 0, count), swap(send_b, 1, count)


def second_swap(parts, got, count):
    keep_a, _, keep_b, _ = parts
    got_a, got_b = got
    half = keep_a.shape[0] // 2
    next_a = add(keep_a[half:], got_a[half:])
    next_b = add(keep_b[half:], got_b[half:])
    got_a2, got_b2 = swap(next_a, 1, count), swap(next_b, 0, count)
    keep_a = add(keep_a[:half], got_a[:half])
    keep_b = add(keep_b[:half], got_b[:half])
    return keep_a, keep_b, got_a2, got_b2


def joined(terms):
    keep_a, keep_b, got_a, got_b = terms
    return (
        jnp.concatenate([keep_a, keep_b], axis=1),
        jnp.concatenate([got_a, got_b], axis=1),
    )


def halve(terms, bit, count):
    keep, got = terms
    half = keep.shape[0] // 2
    arrived = swap(add(keep[half:], got[half:]), bit, count)
    return add(keep[:half], got[:half]), arrived


def double(rows, bit, count):
    return jnp.concatenate([rows, swap(rows, bit, count)], axis=0)


def gather_half(rows, split, count):
    return double(rows[:, :split], 1, count), double(rows[:, split:], 0, count)


def gather_last(low, count):
    low_a, low_b = low
    return [low_a, swap(low_a, 0, count)], [low_b, swap(low_b, 1, count)]


def body(
    queries, latent, value_up, out_proj, residual, norm_gain, routes, gates, w_gate, w_up, w_down
):
    slabs = lax.axis_size("ctx")
    senders = lax.axis_size("exp")
    bits = bits_of(senders)
    block, width = residual.shape
    top = routes.shape[1]
    expert_count = senders * w_gate.shape[0]
    capacity = max(2, 3 * block * top // (2 * expert_count))
    orders = (list(range(bits)), [1, 0, *range(2, bits)])
    tiles = width // (2 * LANES)
    low = LANES * (tiles * first_share // 28)
    halves = (low, LANES * tiles - low)
    place = jnp.stack([lax.axis_index("ctx"), lax.axis_index("exp")]).astype(jnp.int32)

    keys = shifted(latent.T, slabs)
    arrived, gate_source, up_source = tie(keys[1:], w_gate, w_up)
    keys = [keys[0], *arrived]
    gate_others = shifted(gate_source, slabs)[1:]
    up_others = shifted(up_source, slabs)[1:]

    hva, hvb, *parts = attend_project(
        place, queries, keys, value_up, out_proj, halves[0], block, orders
    )
    more = project_more(hva, hvb, out_proj, 2 * halves[0], halves[1])
    gain = norm_gain.astype(f32)
    inner_bits = list(range(2, bits))

    def finished(terms, c):
        keep, got = terms
        cols = slice(2 * halves[0] * c, 2 * (halves[0] + halves[1] * c))
        rows = (residual[:, cols].astype(f32) + (keep.astype(f32) + got.astype(f32))).astype(bf16)
        wide = rows.astype(f32)
        return (
            rows,
            (wide * gain[None, cols]).astype(bf16),
            jnp.sum(wide * wide, axis=1, keepdims=True),
        )

    got = first_swap(parts, senders)
    got, more, gate_others, up_others, down_source = tie(got, more, gate_others, up_others, w_down)
    terms = second_swap(parts, got, senders)
    got = first_swap(more, senders)
    ahead, rest = joined(terms), inner_bits[:-1]
    for bit in rest:
        ahead = halve(ahead, bit, senders)
    got, _ = tie(got, ahead)
    down_others = shifted(down_source, slabs)[1:]

    behind = second_swap(more, got, senders)
    ahead = halve(ahead, inner_bits[-1], senders)
    hidden_0, payload, squares_0 = finished(ahead, 0)
    behind = joined(behind)
    for bit in inner_bits[:-1]:
        behind = halve(behind, bit, senders)
    payload = double(payload, inner_bits[-1], senders)
    behind = halve(behind, inner_bits[-1], senders)
    for bit in inner_bits[-2::-1]:
        payload = double(payload, bit, senders)
    behind, down_others = tie(behind, down_others)
    hidden_1, rows, squares_1 = finished(behind, 1)
    inverse = lax.rsqrt((squares_0 + squares_1) / width + norm_epsilon)
    coarse = lax.reduce_precision(inverse, 8, 7)
    meta = jnp.concatenate(
        [
            routes.astype(bf16),
            gates.astype(bf16),
            coarse.astype(bf16),
            (inverse - coarse).astype(bf16),
            jnp.zeros((block, LANES - 2 * top - 2), bf16),
        ],
        axis=1,
    )
    rows = jnp.concatenate([rows, meta], axis=1)

    gate_parts = [w_gate, *gate_others]
    up_parts = [w_up, *up_others]
    down_parts = [w_down, *down_others]
    low = gather_half(payload, halves[0], senders)
    for bit in inner_bits[::-1]:
        rows = double(rows, bit, senders)
    a, b = gather_last(low, senders)
    low = gather_half(rows, halves[1], senders)
    a, b, low = tie(a, b, low)
    base = gate_up(a, b, gate_parts, up_parts)
    a, b = gather_last(low, senders)
    slots = finish(
        place, a, b, base, gate_parts, up_parts, down_parts, 2 * halves[0], block, orders[0], top, senders, capacity
    )
    expert_out = slots.reshape(capacity, senders, width).transpose(1, 0, 2)[None, None]
    return jnp.concatenate([hidden_0, hidden_1], axis=1), expert_out


def solution(mesh):
    placed = (
        P("ctx", "exp"),
        P("ctx", None),
        P("exp", None, None),
        P("exp", None),
        P(("ctx", "exp"), None),
        P(),
        P(("ctx", "exp"), None),
        P(("ctx", "exp"), None),
        P("exp", None, "ctx"),
        P("exp", None, "ctx"),
        P("exp", "ctx", None),
    )
    return jax.shard_map(
        body,
        mesh=mesh,
        in_specs=placed,
        out_specs=(P(("ctx", "exp"), None), P("ctx", "exp", None, None, None)),
        check_vma=False,
    )
```
